512 devices in a mesh: az: 32 (over z, y_lo), rad: 8 (over x, core), tool: 2 (over y_hi).
Axes of the slice: x: 4, y: 4 (y_hi: 2, y_lo: 2; y = y_hi * 2 + y_lo), z: 16, core: 2. Of those that a mesh axis runs over, the one named last changes fastest.
Arguments:
- dwell: float32 [4, 256, 32768], P('tool', 'rad', 'az'), may hold values from -6 to 6
- residual: float32 [256, 32768], P('rad', 'az')
- influence: bfloat16 [4, 64, 64], P('tool')
- cycle_start: int32 [256], P('rad'), may hold values from 0 to 8191
- cycle_end: int32 [256], P('rad'), may hold values from 24577 to 32768
- allowed_bits: int32 [4, 256, 2048], P('tool', 'rad', 'az'), may hold values from 0 to 65535
Outputs:
- dwell_new: float32 [4, 256, 32768], P('tool', 'rad', 'az')
- residual_new: float32 [256, 32768], P('rad', ('az', 'tool'))
- direction_new: float32 [4, 256, 32768], P('tool', 'rad', 'az')
The draws below stay inside these ranges and needn't reach their ends.
All inputs are finite; a program needn't handle non-finite values.
Results may differ from the reference program's by a relative error of at most 0.0003.
Values may be sent and summed in bfloat16 or wider, within the bound.
A program may use at most 64 MiB of HBM per device.

```python
import math
import jax
import jax.numpy as jnp
from jax import lax

KS = 64
HALF = 32
TOOLS = 4
CYCLES = 256
AZ = 32768
WORDS = 2048


def draw_residual(key, part):
    keys = jax.random.split(key, 5)
    cycle_pos = jnp.arange(CYCLES, dtype=jnp.float32)[:, None]
    az_pos = jnp.arange(AZ, dtype=jnp.float32)[None, :]
    cycle_scale = jnp.power(10.0, cycle_pos / (CYCLES - 1) - 0.5)
    az_scale = jnp.power(10.0, 0.5 * az_pos / (AZ - 1) - 0.25)
    rough = 0.7 * jax.random.normal(keys[0], (CYCLES, AZ), jnp.float32)
    amounts = 0.6 * jax.random.normal(keys[1], (4,), jnp.float32)
    beside_all = jax.random.randint(keys[2], (4,), 1, 17).astype(jnp.float32)
    across = jax.random.randint(keys[3], (4,), 1, 5).astype(jnp.float32)
    phases = jax.random.uniform(keys[4], (4,), jnp.float32, -math.pi, math.pi)
    smooth = jnp.zeros((CYCLES, AZ), jnp.float32)
    for number in range(4):
        smooth = smooth + amounts[number] * jnp.sin(2.0 * math.pi * beside_all[number] * az_pos / AZ + math.pi * across[number] * cycle_pos / CYCLES + phases[number])
    return (cycle_scale * az_scale * (rough + smooth)).astype(jnp.float32)


def draw_influence(key, part):
    tool_pos = jnp.arange(TOOLS, dtype=jnp.float32)[:, None, None]
    amplitude = jnp.power(6.0, tool_pos / (2.0 * max(TOOLS - 1, 1)))
    entries = jax.random.uniform(key, (TOOLS, KS, KS), jnp.float32, 0.25, 1.0)
    return (amplitude * entries / (KS * KS)).astype(jnp.bfloat16)


def with_ends(values, key, smallest, high):
    place = [jax.random.randint(jax.random.fold_in(key, axis), (), 0, length) for axis, length in enumerate(values.shape)]
    longest = values.shape.index(max(values.shape))
    beside = place[:longest] + [(place[longest] + 1) % values.shape[longest]] + place[longest + 1:]
    return values.at[tuple(place)].set(smallest).at[tuple(beside)].set(high)


def levels(stream_key, shape, pieces, low, largest):
    factor_of = 1.0
    for axis_at, parts in pieces:
        steps = jax.random.uniform(jax.random.fold_in(jax.random.fold_in(stream_key, 6), axis_at), (parts,), jnp.float32, low / len(pieces), largest / len(pieces))
        factor_of = factor_of * jnp.repeat(jnp.exp(steps), shape[axis_at] // parts).reshape((-1,) + (1,) * (len(shape) - 1 - axis_at))
    return factor_of


def bell_draw(own_key, dims, scale, reach, cuts=(), kind=jnp.bfloat16):
    values = scale * jax.random.normal(own_key, dims, jnp.float32)
    if cuts:
        values = values * levels(own_key, dims, cuts, -0.22, 0.18)
    return jnp.clip(values, -reach, reach).astype(kind)


def setup_inputs(seed: int = 0) -> dict:
    arg_keys = jax.random.split(jax.random.key(seed), 7)
    dwell = bell_draw(arg_keys[0], (TOOLS, CYCLES, AZ), 1.0, 6.0, ((0, 2), (1, 8), (2, 32)), jnp.float32)
    residual = draw_residual(jax.random.fold_in(arg_keys[6], 71), 0)
    influence = draw_influence(jax.random.fold_in(arg_keys[6], 71), 0)
    cycle_start = with_ends(jax.random.randint(arg_keys[3], (CYCLES,), 0, AZ // 4), jax.random.fold_in(arg_keys[3], 1), 0, (AZ // 4) - 1).astype(jnp.int32)
    cycle_end = with_ends(jax.random.randint(arg_keys[4], (CYCLES,), 3 * AZ // 4 + 1, AZ + 1), jax.random.fold_in(arg_keys[4], 1), 3 * AZ // 4 + 1, AZ).astype(jnp.int32)
    allowed_bits = with_ends(jax.random.randint(arg_keys[5], (TOOLS, CYCLES, WORDS), 0, 65536), jax.random.fold_in(arg_keys[5], 1), 0, 65535).astype(jnp.int32)
    return dict(dwell=dwell, residual=residual, influence=influence, cycle_start=cycle_start, cycle_end=cycle_end, allowed_bits=allowed_bits)


EPSILON = 1e-6


def unpack_bits(allowed_bits):
    bit_shift = jnp.arange(AZ, dtype=jnp.int32) % 16
    return ((jnp.repeat(allowed_bits, 16, axis=2) >> bit_shift) & 1).astype(jnp.float32)


def valid_region(cycle_start, cycle_end):
    columns = jnp.arange(AZ, dtype=jnp.int32)[None, :]
    return ((columns >= cycle_start[:, None]) & (columns < cycle_end[:, None])).astype(jnp.float32)


def wrapped_cycles(values):
    cycle_pad = jnp.pad(values, ((0, 0), (HALF, HALF), (0, 0)))
    return jnp.concatenate([cycle_pad[:, :, AZ - HALF:], cycle_pad, cycle_pad[:, :, :HALF]], axis=2)


def lowered(values):
    return lax.optimization_barrier(values.astype(jnp.bfloat16))


def forward_removal(direction_low, kernel):
    padded = wrapped_cycles(direction_low.astype(jnp.float32))[None]
    padded = padded[:, :, :CYCLES + KS - 1, :AZ + KS - 1]
    result = lax.conv_general_dilated(padded, kernel[None], (1, 1), "VALID", precision=lax.Precision.HIGHEST)
    return result[0, 0]


def adjoint_removal(field_low, kernel):
    padded = wrapped_cycles(field_low.astype(jnp.float32)[None])[None]
    padded = padded[:, :, 1:, 1:]
    flipped = kernel[:, None, ::-1, ::-1]
    result = lax.conv_general_dilated(padded, flipped, (1, 1), "VALID", precision=lax.Precision.HIGHEST)
    return result[0]


def reference(dwell, residual, influence, cycle_start, cycle_end, allowed_bits):
    inside = valid_region(cycle_start, cycle_end)
    allowed = unpack_bits(allowed_bits)
    kernel = influence.astype(jnp.float32)
    first_low = lowered(inside * residual)
    gradient = allowed * adjoint_removal(first_low, kernel)
    gamma = jnp.sum(gradient * gradient)
    direction_low = lowered(gradient)
    removal = inside * forward_removal(direction_low, kernel)
    curvature = jnp.sum(removal * removal)
    step_size = gamma / (curvature + EPSILON)
    dwell_new = dwell + step_size * gradient
    residual_new = residual - step_size * removal
    second_low = lowered(inside * residual_new)
    gradient_new = allowed * adjoint_removal(second_low, kernel)
    gamma_new = jnp.sum(gradient_new * gradient_new)
    direction_new = gradient_new + (gamma_new / (gamma + EPSILON)) * gradient
    return (dwell_new, residual_new, direction_new)
```

```python
import jax
import jax.numpy as jnp
from jax import lax
from jax.experimental import pallas as pl
from jax.experimental.pallas import tpu as pltpu
from jax.sharding import PartitionSpec as P

EPSILON = 1e-06
MESH = pl.DeviceIdType.MESH
F32 = jnp.float32
BF16 = jnp.bfloat16
LANES = 128
SUB = 8


def build(dwell_shape, influence_shape, words, az_count, rad_count, tool_count):
    tools, rows, width = dwell_shape
    extent = influence_shape[-1]
    tiles = width // LANES
    assert tiles == SUB and extent == 64 and rows == 32
    pairs = rows // 2
    field = rows * tiles
    steps = extent // 2 + 1
    group_count = rad_count * tool_count
    share = width // tool_count
    share_tiles = share // LANES

    def body(
        dwell_hbm,
        residual_hbm,
        influence_ref,
        start_ref,
        end_ref,
        bits_ref,
        dwell_out,
        residual_out,
        direction_out,
        natural,
        dwell_v,
        whole,
        masked,
        masked_edge,
        masked_edge_out,
        low_out,
        low_edge_out,
        low_in,
        low_edge_in,
        inside,
        allowed,
        head_adj,
        head_fwd,
        head_two,
        keep,
        band_adj,
        band_fwd,
        win_adj,
        win_fwd,
        acc,
        acc_fwd,
        gradient,
        grad_low,
        grad_edge_out,
        grad_in,
        grad_edge_in,
        part,
        part_in,
        removal,
        removal_edge_out,
        removal_edge,
        edge,
        gradient_new,
        dwell_res,
        residual_res,
        direction_res,
        msg,
        box_a,
        box_b,
        local_sem,
        halo_send,
        halo_recv,
        tool_sem,
        sum_send,
        sum_recv,
    ):
        az, rad, tool = lax.axis_index("az"), lax.axis_index("rad"), lax.axis_index("tool")
        lane = lax.broadcasted_iota(jnp.int32, (SUB, LANES), 1)
        sub = lax.broadcasted_iota(jnp.int32, (SUB, LANES), 0)
        left_half = lane < LANES // 2

        residual_copy = pltpu.make_async_copy(residual_hbm, natural, local_sem.at[0])
        residual_copy.start()
        dwell_copy = pltpu.make_async_copy(dwell_hbm, dwell_v, local_sem.at[1])
        dwell_copy.start()

        def at(dr, da):
            return {
                "az": lax.rem(az + da + az_count, az_count),
                "rad": rad + dr,
                "tool": tool,
            }

        def group_peer(step):
            peer = lax.rem(rad * tool_count + tool + step, group_count)
            return {"az": az, "rad": peer // tool_count, "tool": lax.rem(peer, tool_count)}

        def ring_peer(step):
            return {"az": lax.rem(az + step, az_count), "rad": rad, "tool": tool}

        has_up, has_down = rad > 0, rad < rad_count - 1

        barrier = pltpu.get_barrier_semaphore()

        def greet(peer):
            pl.semaphore_signal(barrier, inc=1, device_id=peer, device_id_type=MESH)

        @pl.loop(1, group_count)
        def _(step):
            greet(group_peer(step))

        @pl.loop(1, az_count)
        def _(step):
            greet(ring_peer(step))

        @pl.when(has_up)
        def _():
            greet(at(-1, -1))
            greet(at(-1, 1))

        @pl.when(has_down)
        def _():
            greet(at(1, -1))
            greet(at(1, 1))

        residual_copy.wait()
        for c in range(tiles):
            whole[pl.ds(c, rows, stride=tiles), :] = natural[:, c * LANES : (c + 1) * LANES]
        column = az * width + sub * LANES + lane

        @pl.loop(0, rows)
        def _(r):
            at_r = pl.ds(pl.multiple_of(r * tiles, tiles), tiles)
            valid = ((column >= start_ref[r]) & (column < end_ref[r])).astype(F32)
            inside[at_r, :] = valid
            masked[1, at_r, :] = valid * whole[at_r, :]

        low_out[...] = masked[1].astype(BF16)
        for side, tile in ((0, tiles - 1), (1, 0)):
            tile_of = masked[1, pl.ds(tile, rows, stride=tiles), :]
            masked_edge_out[side] = tile_of
            low_edge_out[side] = tile_of.astype(BF16)

        extra = 2 * (has_up.astype(jnp.int32) + has_down.astype(jnp.int32))
        pl.semaphore_wait(barrier, group_count + az_count - 2 + extra)

        def halo(phase, mid_src, mid_dst, edge_src, edge_dst):
            copies = []
            for d in (0, 2, 1):
                for side, da in ((1, 0), (0, 1), (2, -1)):
                    if d == 1 and side == 1:
                        continue
                    src = mid_src if side == 1 else edge_src.at[side // 2]
                    dst = mid_dst.at[d] if side == 1 else edge_dst.at[d, side // 2]
                    copy = pltpu.make_async_remote_copy(
                        src_ref=src,
                        dst_ref=dst,
                        send_sem=halo_send.at[phase, 3 * d + side],
                        recv_sem=halo_recv.at[phase, 3 * d + side],
                        device_id=at(1 - d, da),
                        device_id_type=MESH,
                    )
                    copies.append((d, copy))

            def start():
                for d, copy in copies:
                    if d == 1:
                        copy.start()
                    else:
                        pl.when(has_down if d == 0 else has_up)(copy.start)

            def wait_recv():
                for d, copy in copies:
                    if d == 1:
                        copy.wait_recv()
                    else:
                        pl.when(has_up if d == 0 else has_down)(copy.wait_recv)

            def wait_send():
                for d, copy in copies:
                    if d == 1:
                        copy.wait_send()
                    else:
                        pl.when(has_down if d == 0 else has_up)(copy.wait_send)

            return start, wait_recv, wait_send

        first_halo = halo(0, low_out, low_in, low_edge_out, low_edge_in)
        masked_halo = halo(1, masked.at[1], masked, masked_edge_out, masked_edge)
        grad_halo = halo(2, grad_low, grad_in, grad_edge_out, grad_edge_in)
        removal_halo = halo(3, removal.at[1], removal, removal_edge_out, removal_edge)

        first_halo[0]()

        j_of = lax.broadcasted_iota(jnp.int32, (extent, LANES), 0)
        l_of = lax.broadcasted_iota(jnp.int32, (extent, LANES), 1)

        def spread(rows_of, where_j):
            return jnp.dot(rows_of, (l_of == where_j).astype(BF16), preferred_element_type=F32)

        head_adj[...] = spread(influence_ref[0], j_of) + spread(influence_ref[1], extent + j_of)
        head_fwd[...] = jnp.zeros_like(head_fwd)
        head_two[...] = jnp.zeros_like(head_two)
        for t in range(tools):
            head_fwd[t, 0:extent, :] = spread(influence_ref[t], extent - 1 - j_of)
            head_two[t, 1 : extent + 1, :] = spread(influence_ref[t], 2 * extent - 1 - j_of)
        head_fwd[...] = head_fwd[...] + head_two[...]
        c_of = lax.broadcasted_iota(jnp.int32, (LANES, LANES), 0)
        o_of = lax.broadcasted_iota(jnp.int32, (LANES, LANES), 1)
        low_side = o_of < extent
        off = o_of - c_of
        adj_keep = (low_side & (off >= -extent) & (off < 0)) | (~low_side & (off >= 0) & (off < extent))
        fwd_keep = (low_side & (off > -extent) & (off <= 0)) | (~low_side & (off > 0) & (off <= extent))
        keep[0] = adj_keep.astype(F32)
        keep[1] = fwd_keep.astype(F32)
        blank = jnp.zeros((LANES, LANES), BF16)
        band_adj[0:LANES, :] = blank
        band_adj[LANES : 2 * LANES, :] = blank
        band_adj[(extent + 2) * LANES : (extent + 3) * LANES, :] = blank
        for t in range(tools):
            band_fwd[t, (extent + 1) * LANES : (extent + 2) * LANES, :] = blank

        def toeplitz(head, shift, which):
            square = jnp.broadcast_to(head, (LANES, LANES))
            turned = pltpu.roll(square, shift, axis=1, stride=1, stride_axis=0)
            return (turned * keep[which]).astype(BF16)

        @pl.loop(0, extent)
        def _(i):
            at_i = pl.ds(pl.multiple_of((extent + 1 - i) * LANES, LANES), LANES)
            band_adj[at_i, :] = toeplitz(head_adj[pl.ds(i, 1), :], extent, 0)

        k_of = lax.broadcasted_iota(jnp.int32, (words, LANES), 0)
        b_of = lax.broadcasted_iota(jnp.int32, (words, LANES), 1)
        word = bits_ref[...].reshape(tools * rows, words)
        low_byte = (word & 255).astype(F32).astype(BF16)
        high_byte = (word >> 8).astype(F32).astype(BF16)
        for c in range(tiles):
            mine = k_of == c * (LANES // 16) + b_of // 16
            upper = b_of % 16 >= 8
            byte = jnp.dot(low_byte, (mine & ~upper).astype(BF16), preferred_element_type=F32)
            byte += jnp.dot(high_byte, (mine & upper).astype(BF16), preferred_element_type=F32)
            bit_at = lax.broadcasted_iota(jnp.int32, byte.shape, 1) % 8
            allowed[pl.ds(c, tools * rows, stride=tiles), :] = (
                (byte.astype(jnp.int32) >> bit_at) & 1
            ).astype(F32)

        def assemble(target, d, two_rows):
            @pl.loop(0, pairs)
            def _(m):
                both = two_rows(m)
                for a in range(2):
                    row = both[a * tiles : (a + 1) * tiles]
                    before = jnp.broadcast_to(edge[0, pl.ds(2 * m + a, 1), :], (SUB, LANES))
                    after = jnp.broadcast_to(edge[1, pl.ds(2 * m + a, 1), :], (SUB, LANES))
                    prior = jnp.where(sub == 0, before, pltpu.roll(row, 1, axis=0))
                    later = jnp.where(sub == SUB - 1, after, pltpu.roll(row, SUB - 1, axis=0))
                    even = pltpu.roll(jnp.where(lane >= 96, prior, row), 32, axis=1)
                    odd = pltpu.roll(jnp.where(lane < 32, later, row), 96, axis=1)
                    target[
                        pl.ds(pl.multiple_of((pairs * d + m) * 16, 16), 16),
                        a * LANES : (a + 1) * LANES,
                    ] = jnp.concatenate([even, odd], axis=0).astype(BF16)

        def at_pair(m):
            return pl.ds(pl.multiple_of(m * 2 * tiles, 2 * tiles), 2 * tiles)

        def fill_blank(target, d):
            target[d * pairs * 16 : (d + 1) * pairs * 16, :] = jnp.zeros((pairs * 16, 2 * LANES), BF16)

        def over_blocks(block, blank_of=None):
            block(1)
            for d, there in ((0, has_up), (2, has_down)):
                pl.when(there)(lambda d=d: block(d))
                if blank_of is not None:
                    pl.when(jnp.logical_not(there))(lambda d=d: blank_of(d))

        def adjoint(out):
            acc[...] = jnp.zeros_like(acc)

            @pl.loop(0, steps // 3)
            def _(kk):
                lhs = jnp.concatenate(
                    [
                        win_adj[pl.ds(pl.multiple_of((3 * kk + u) * 16, 16), pairs * 16), :]
                        for u in range(3)
                    ],
                    axis=1,
                )
                first = pl.multiple_of(6 * kk * LANES, LANES)
                rhs = jnp.concatenate(
                    [
                        band_adj[pl.ds(first + LANES, 6 * LANES), :],
                        band_adj[pl.ds(first, 6 * LANES), :],
                    ],
                    axis=1,
                )
                acc[...] += jnp.dot(lhs, rhs, preferred_element_type=F32)

            def finish(m, total):
                for b in range(2):
                    cols = slice(b * LANES, (b + 1) * LANES)
                    even = acc[pl.ds(pl.multiple_of(m * 16, 16), 8), cols]
                    odd = acc[pl.ds(pl.multiple_of(m * 16 + 8, 8), 8), cols]
                    values = (
                        jnp.where(left_half, even, pltpu.roll(odd, 64, axis=1)),
                        jnp.where(left_half, pltpu.roll(even, 64, axis=1), odd),
                    )
                    for t in range(tools):
                        at_r = pl.ds(pl.multiple_of((t * rows + 2 * m + b) * tiles, tiles), tiles)
                        value = allowed[at_r, :] * values[t]
                        out[at_r, :] = value
                        total = total + value * value
                return total

            return lax.fori_loop(0, pairs, finish, jnp.zeros((SUB, LANES), F32))

        def sum_stage(which, source, box, count, peer_of):
            def copy_to(step):
                return pltpu.make_async_remote_copy(
                    src_ref=msg.at[source],
                    dst_ref=box.at[step - 1],
                    send_sem=sum_send.at[which],
                    recv_sem=sum_recv.at[which],
                    device_id=peer_of(step),
                    device_id_type=MESH,
                )

            @pl.loop(1, count)
            def _(step):
                copy_to(step).start()

            all_of = pltpu.make_async_remote_copy(
                src_ref=box,
                dst_ref=box,
                send_sem=sum_send.at[which],
                recv_sem=sum_recv.at[which],
                device_id=peer_of(1),
                device_id_type=MESH,
            )
            return all_of

        def total_of(first, side_work):
            stage = sum_stage(first, first, box_a.at[first // 2], group_count, group_peer)
            side_work()
            stage.wait_recv()
            msg[first + 1] = msg[first] + jnp.sum(box_a[first // 2], axis=0)
            other = sum_stage(first + 1, first + 1, box_b.at[first // 2], az_count, ring_peer)
            other.wait_recv()
            everything = msg[first + 1] + jnp.sum(box_b[first // 2], axis=0)
            return jnp.sum(everything, axis=1, keepdims=True), (stage, other)

        first_halo[1]()

        def first_block(d):
            if d == 1:
                edge[...] = low_edge_in[1].astype(F32)
                assemble(win_adj, 1, lambda m: masked[1, at_pair(m), :])
            else:
                edge[...] = low_edge_in[d].astype(F32)
                assemble(win_adj, d, lambda m: low_in[d, at_pair(m), :].astype(F32))

        over_blocks(first_block, lambda d: fill_blank(win_adj, d))
        masked_halo[0]()
        gamma_part = adjoint(gradient)
        grad_low[...] = gradient[...].astype(BF16)
        for side, tile in ((0, tiles - 1), (1, 0)):
            grad_edge_out[side] = gradient[pl.ds(tile, tools * rows, stride=tiles), :].astype(BF16)
        grad_halo[0]()

        for t in range(tools):

            @pl.loop(0, extent + 1)
            def _(q, t=t):
                at_q = pl.ds(pl.multiple_of(q * LANES, LANES), LANES)
                band_fwd[t, at_q, :] = toeplitz(head_fwd[t, pl.ds(q, 1), :], extent + 1, 1)

        grad_halo[1]()

        def grad_block(d):
            for t in range(tools):
                edge[...] = grad_edge_in[d, :, t * rows : (t + 1) * rows, :].astype(F32)
                first = t * field
                if d == 1:
                    assemble(win_fwd.at[t], 1, lambda m, first=first: gradient[pl.ds(pl.multiple_of(first + m * 16, 16), 16), :])
                else:
                    assemble(
                        win_fwd.at[t],
                        d,
                        lambda m, first=first: grad_in[
                            d, pl.ds(pl.multiple_of(first + m * 16, 16), 16), :
                        ].astype(F32),
                    )

        def grad_blank(d):
            for t in range(tools):
                fill_blank(win_fwd.at[t], d)

        over_blocks(grad_block, grad_blank)

        acc_fwd[...] = jnp.zeros_like(acc_fwd)

        @pl.loop(0, steps // 3)
        def _(kk):
            lhs = jnp.concatenate(
                [
                    win_fwd[t, pl.ds(pl.multiple_of((3 * kk + u) * 16, 16), pairs * 16), :]
                    for t in range(tools)
                    for u in range(3)
                ],
                axis=1,
            )
            first = pl.multiple_of(6 * kk * LANES, LANES)
            rhs = jnp.concatenate(
                [band_fwd[t, pl.ds(first, 6 * LANES), :] for t in range(tools)], axis=0
            )
            acc_fwd[...] += jnp.dot(lhs, rhs, preferred_element_type=F32)

        @pl.loop(0, pairs)
        def _(m):
            even = acc_fwd[pl.ds(pl.multiple_of(m * 16, 16), 8), :]
            odd = acc_fwd[pl.ds(pl.multiple_of(m * 16 + 8, 8), 8), :]
            top = jnp.where(left_half, even, pltpu.roll(odd, 64, axis=1))
            low = jnp.where(left_half, pltpu.roll(even, 64, axis=1), odd)
            at_m = at_pair(m)
            part[at_m, :] = inside[at_m, :] * jnp.concatenate([top, low], axis=0)

        tool_copies = []
        for step in range(1, tool_count):
            tool_copies.append(
                pltpu.make_async_remote_copy(
                    src_ref=part,
                    dst_ref=part_in.at[step - 1],
                    send_sem=tool_sem.at[0, step - 1],
                    recv_sem=tool_sem.at[1, step - 1],
                    device_id={"az": az, "rad": rad, "tool": lax.rem(tool + step, tool_count)},
                    device_id_type=MESH,
                )
            )
        for copy in tool_copies:
            copy.start()
        for copy in tool_copies:
            copy.wait_recv()

        def join(m, total):
            at_m = at_pair(m)
            value = part[at_m, :]
            for step in range(1, tool_count):
                value = value + part_in[step - 1, at_m, :]
            removal[1, at_m, :] = value
            return total + value[:SUB] * value[:SUB] + value[SUB:] * value[SUB:]

        curvature_part = lax.fori_loop(0, pairs, join, jnp.zeros((SUB, LANES), F32))
        for side, tile in ((0, tiles - 1), (1, 0)):
            removal_edge_out[side] = removal[1, pl.ds(tile, rows, stride=tiles), :]
        msg[0] = jnp.concatenate(
            [
                jnp.sum(gamma_part, axis=0, keepdims=True),
                jnp.sum(curvature_part, axis=0, keepdims=True),
            ],
            axis=0,
        )

        def beside():
            removal_halo[0]()
            masked_halo[1]()
            removal_halo[1]()
            dwell_copy.wait()

        sums, stages = total_of(0, beside)
        gamma = sums[0:1]
        curvature = sums[1:2] * (1.0 / tool_count)
        step_size = gamma / (curvature + EPSILON)

        def second_block(d):
            edge[...] = masked_edge[d] - step_size * removal_edge[d]
            assemble(
                win_adj, d, lambda m: masked[d, at_pair(m), :] - step_size * removal[d, at_pair(m), :]
            )

        over_blocks(second_block)
        new_part = adjoint(gradient_new)
        new_row = jnp.sum(new_part, axis=0, keepdims=True)
        msg[2] = jnp.concatenate([new_row, new_row], axis=0)

        dwell_store = pltpu.make_async_copy(dwell_res, dwell_out, local_sem.at[2])
        residual_store = pltpu.make_async_copy(residual_res, residual_out, local_sem.at[3])
        direction_store = pltpu.make_async_copy(direction_res, direction_out, local_sem.at[4])

        def outputs():
            for t in range(tools):
                for c in range(tiles):
                    cols = slice(c * LANES, (c + 1) * LANES)
                    step_of = gradient[pl.ds(t * field + c, rows, stride=tiles), :]
                    dwell_res[t, :, cols] = dwell_v[t, :, cols] + step_size * step_of
            dwell_store.start()
            for c in range(share_tiles):
                from_c = pl.ds(tool * share_tiles + c, rows, stride=tiles)
                residual_res[:, c * LANES : (c + 1) * LANES] = (
                    whole[from_c, :] - step_size * removal[1, from_c, :]
                )
            residual_store.start()

        new_sums, new_stages = total_of(2, outputs)
        ratio = new_sums[0:1] / (gamma + EPSILON)
        for t in range(tools):
            for c in range(tiles):
                cols = slice(c * LANES, (c + 1) * LANES)
                from_c = pl.ds(t * field + c, rows, stride=tiles)
                direction_res[t, :, cols] = gradient_new[from_c, :] + ratio * gradient[from_c, :]
        direction_store.start()

        for phase in (first_halo, masked_halo, grad_halo, removal_halo):
            phase[2]()
        for copy in tool_copies:
            copy.wait_send()
        for stage in stages + new_stages:
            stage.wait_send()
        dwell_store.wait()
        residual_store.wait()
        direction_store.wait()

    any_spec = pl.BlockSpec(memory_space=pl.ANY)
    vmem_spec = pl.BlockSpec(memory_space=pltpu.VMEM)
    smem_spec = pl.BlockSpec(memory_space=pltpu.SMEM)
    scratch = [
        ((rows, width), F32),
        (dwell_shape, F32),
        ((field, LANES), F32),
        ((3, field, LANES), F32),
        ((3, 2, rows, LANES), F32),
        ((2, rows, LANES), F32),
        ((field, LANES), BF16),
        ((2, rows, LANES), BF16),
        ((3, field, LANES), BF16),
        ((3, 2, rows, LANES), BF16),
        ((field, LANES), F32),
        ((tools * field, LANES), F32),
        ((extent, LANES), F32),
        ((tools, extent + 8, LANES), F32),
        ((tools, extent + 8, LANES), F32),
        ((2, LANES, LANES), F32),
        (((extent + 3) * LANES, LANES), BF16),
        ((tools, (extent + 2) * LANES, LANES), BF16),
        ((3 * pairs * 16, 2 * LANES), BF16),
        ((tools, 3 * pairs * 16, 2 * LANES), BF16),
        ((pairs * 16, 2 * LANES), F32),
        ((pairs * 16, LANES), F32),
        ((tools * field, LANES), F32),
        ((tools * field, LANES), BF16),
        ((2, tools * rows, LANES), BF16),
        ((3, tools * field, LANES), BF16),
        ((3, 2, tools * rows, LANES), BF16),
        ((field, LANES), F32),
        ((tool_count - 1, field, LANES), F32),
        ((3, field, LANES), F32),
        ((2, rows, LANES), F32),
        ((3, 2, rows, LANES), F32),
        ((2, rows, LANES), F32),
        ((tools * field, LANES), F32),
        (dwell_shape, F32),
        ((rows, share), F32),
        (dwell_shape, F32),
        ((4, 2, LANES), F32),
        ((2, group_count - 1, 2, LANES), F32),
        ((2, az_count - 1, 2, LANES), F32),
    ]
    return pl.pallas_call(
        body,
        out_shape=(
            jax.ShapeDtypeStruct(dwell_shape, F32),
            jax.ShapeDtypeStruct((rows, share), F32),
            jax.ShapeDtypeStruct(dwell_shape, F32),
        ),
        in_specs=[any_spec, any_spec, vmem_spec, smem_spec, smem_spec, vmem_spec],
        out_specs=(any_spec, any_spec, any_spec),
        scratch_shapes=[pltpu.VMEM(shape, dtype) for shape, dtype in scratch]
        + [
            pltpu.SemaphoreType.DMA((5,)),
            pltpu.SemaphoreType.DMA((4, 9)),
            pltpu.SemaphoreType.DMA((4, 9)),
            pltpu.SemaphoreType.DMA((2, max(tool_count - 1, 1))),
            pltpu.SemaphoreType.DMA((4,)),
            pltpu.SemaphoreType.DMA((4,)),
        ],
        compiler_params=pltpu.CompilerParams(
            collective_id=0, has_side_effects=True, vmem_limit_bytes=40 * 1024 * 1024
        ),
        name="cgls",
    )


def solution(mesh):
    def per_device(dwell, residual, influence, cycle_start, cycle_end, allowed_bits):
        call = build(
            dwell.shape,
            influence.shape,
            allowed_bits.shape[-1],
            mesh.shape["az"],
            mesh.shape["rad"],
            mesh.shape["tool"],
        )
        return call(dwell, residual, influence, cycle_start, cycle_end, allowed_bits)

    in_specs = (
        P("tool", "rad", "az"),
        P("rad", "az"),
        P("tool", None, None),
        P("rad"),
        P("rad"),
        P("tool", "rad", "az"),
    )
    out_specs = (P("tool", "rad", "az"), P("rad", ("az", "tool")), P("tool", "rad", "az"))
    return jax.shard_map(
        per_device, mesh=mesh, in_specs=in_specs, out_specs=out_specs, check_vma=False
    )
```

```python
import jax
import jax.numpy as jnp
from jax import lax
from jax.experimental import pallas as pl
from jax.experimental.pallas import tpu as pltpu
from jax.sharding import PartitionSpec as P

EPSILON = 1e-06
MESH = pl.DeviceIdType.MESH
F32 = jnp.float32
BF16 = jnp.bfloat16
LANES = 128
SUB = 8


def build(dwell_shape, influence_shape, words, az_count, rad_count, tool_count):
    tools, rows, width = dwell_shape
    extent = influence_shape[-1]
    tiles = width // LANES
    assert tiles == SUB and extent == 64 and rows == 32
    pairs = rows // 2
    field = rows * tiles
    steps = extent // 2 + 1
    plane_count = 2 * rad_count * tool_count
    line_count = az_count // 2
    for count in (az_count, rad_count, tool_count):
        assert count & (count - 1) == 0
    share = width // tool_count
    share_tiles = share // LANES

    def body(
        dwell_hbm,
        residual_hbm,
        influence_hbm,
        start_hbm,
        end_hbm,
        bits_hbm,
        dwell_out,
        residual_out,
        direction_out,
        influence_ref,
        start_ref,
        end_ref,
        bits_ref,
        natural,
        dwell_v,
        whole,
        masked,
        masked_edge,
        masked_edge_out,
        low_out,
        low_edge_out,
        low_in,
        low_edge_in,
        inside,
        allowed,
        head_adj,
        head_fwd,
        head_two,
        keep,
        band_adj,
        band_fwd,
        win_adj,
        win_fwd,
        acc,
        acc_fwd,
        gradient,
        grad_low,
        grad_edge_out,
        grad_in,
        grad_edge_in,
        part,
        part_in,
        removal,
        removal_edge_out,
        removal_edge,
        edge,
        gradient_new,
        dwell_res,
        residual_res,
        direction_res,
        msg,
        box_a,
        box_b,
        local_sem,
        halo_send,
        halo_recv,
        tool_sem,
        sum_send,
        sum_recv,
    ):
        az, rad, tool = lax.axis_index("az"), lax.axis_index("rad"), lax.axis_index("tool")
        lane = lax.broadcasted_iota(jnp.int32, (SUB, LANES), 1)
        sub = lax.broadcasted_iota(jnp.int32, (SUB, LANES), 0)
        left_half = lane < LANES // 2

        residual_copy = pltpu.make_async_copy(residual_hbm, natural, local_sem.at[0])
        start_copy = pltpu.make_async_copy(start_hbm, start_ref, local_sem.at[5])
        end_copy = pltpu.make_async_copy(end_hbm, end_ref, local_sem.at[6])
        influence_copy = pltpu.make_async_copy(influence_hbm, influence_ref, local_sem.at[7])
        bits_copy = pltpu.make_async_copy(bits_hbm, bits_ref, local_sem.at[8])
        dwell_copy = pltpu.make_async_copy(dwell_hbm, dwell_v, local_sem.at[1])
        for copy in (residual_copy, start_copy, end_copy, influence_copy, bits_copy, dwell_copy):
            copy.start()

        def at(dr, da):
            return {
                "az": lax.rem(az + da + az_count, az_count),
                "rad": rad + dr,
                "tool": tool,
            }

        def plane_peer(step):
            return {
                "az": az ^ (step % 2),
                "rad": rad ^ (step // (2 * tool_count)),
                "tool": tool ^ (step // 2 % tool_count),
            }

        def line_peer(step):
            return {"az": az ^ (2 * step), "rad": rad, "tool": tool}

        has_up, has_down = rad > 0, rad < rad_count - 1

        barrier = pltpu.get_barrier_semaphore()

        def greet(peer):
            pl.semaphore_signal(barrier, inc=1, device_id=peer, device_id_type=MESH)

        for step in range(1, plane_count):
            greet(plane_peer(step))
        for step in range(1, line_count):
            greet(line_peer(step))
        outer = 1 - 2 * (1 - lax.rem(az, 2))
        greet(at(0, outer))

        @pl.when(has_up)
        def _():
            greet(at(-1, outer))

        @pl.when(has_down)
        def _():
            greet(at(1, outer))

        residual_copy.wait()
        for c in range(tiles):
            whole[pl.ds(c, rows, stride=tiles), :] = natural[:, c * LANES : (c + 1) * LANES]
        start_copy.wait()
        end_copy.wait()
        column = az * width + sub * LANES + lane

        @pl.loop(0, rows, unroll=4)
        def _(r):
            at_r = pl.ds(pl.multiple_of(r * tiles, tiles), tiles)
            valid = ((column >= start_ref[r]) & (column < end_ref[r])).astype(F32)
            inside[at_r, :] = valid
            masked[1, at_r, :] = valid * whole[at_r, :]

        low_out[...] = masked[1].astype(BF16)
        for side, tile in ((0, tiles - 1), (1, 0)):
            tile_of = masked[1, pl.ds(tile, rows, stride=tiles), :]
            masked_edge_out[side] = tile_of
            low_edge_out[side] = tile_of.astype(BF16)

        extra = 1 + has_up.astype(jnp.int32) + has_down.astype(jnp.int32)
        pl.semaphore_wait(barrier, plane_count + line_count - 2 + extra)

        def halo(phase, mid_src, mid_dst, edge_src, edge_dst):
            copies = []
            for d in (0, 2, 1):
                for side, da in ((1, 0), (0, 1), (2, -1)):
                    if d == 1 and side == 1:
                        continue
                    src = mid_src if side == 1 else edge_src.at[side // 2]
                    dst = mid_dst.at[d] if side == 1 else edge_dst.at[d, side // 2]
                    copy = pltpu.make_async_remote_copy(
                        src_ref=src,
                        dst_ref=dst,
                        send_sem=halo_send.at[phase, 3 * d + side],
                        recv_sem=halo_recv.at[phase, 3 * d + side],
                        device_id=at(1 - d, da),
                        device_id_type=MESH,
                    )
                    copies.append((d, copy))

            def start():
                for d, copy in copies:
                    if d == 1:
                        copy.start()
                    else:
                        pl.when(has_down if d == 0 else has_up)(copy.start)

            def wait_recv():
                for d, copy in copies:
                    if d == 1:
                        copy.wait_recv()
                    else:
                        pl.when(has_up if d == 0 else has_down)(copy.wait_recv)

            def wait_send():
                for d, copy in copies:
                    if d == 1:
                        copy.wait_send()
                    else:
                        pl.when(has_down if d == 0 else has_up)(copy.wait_send)

            return start, wait_recv, wait_send

        first_halo = halo(0, low_out, low_in, low_edge_out, low_edge_in)
        masked_halo = halo(1, masked.at[1], masked, masked_edge_out, masked_edge)
        grad_halo = halo(2, grad_low, grad_in, grad_edge_out, grad_edge_in)
        removal_halo = halo(3, removal.at[1], removal, removal_edge_out, removal_edge)

        first_halo[0]()

        influence_copy.wait()
        j_of = lax.broadcasted_iota(jnp.int32, (extent, LANES), 0)
        l_of = lax.broadcasted_iota(jnp.int32, (extent, LANES), 1)

        def spread(rows_of, where_j):
            return jnp.dot(rows_of, (l_of == where_j).astype(BF16), preferred_element_type=F32)

        head_adj[...] = spread(influence_ref[0], j_of) + spread(influence_ref[1], extent + j_of)
        head_fwd[...] = jnp.zeros_like(head_fwd)
        head_two[...] = jnp.zeros_like(head_two)
        for t in range(tools):
            head_fwd[t, 0:extent, :] = spread(influence_ref[t], extent - 1 - j_of)
            head_two[t, 1 : extent + 1, :] = spread(influence_ref[t], 2 * extent - 1 - j_of)
        head_fwd[...] = head_fwd[...] + head_two[...]
        c_of = lax.broadcasted_iota(jnp.int32, (LANES, LANES), 0)
        o_of = lax.broadcasted_iota(jnp.int32, (LANES, LANES), 1)
        low_side = o_of < extent
        off = o_of - c_of
        adj_keep = (low_side & (off >= -extent) & (off < 0)) | (~low_side & (off >= 0) & (off < extent))
        fwd_keep = (low_side & (off > -extent) & (off <= 0)) | (~low_side & (off > 0) & (off <= extent))
        keep[0] = adj_keep.astype(F32)
        keep[1] = fwd_keep.astype(F32)
        blank = jnp.zeros((LANES, LANES), BF16)
        band_adj[0:LANES, :] = blank
        band_adj[LANES : 2 * LANES, :] = blank
        band_adj[(extent + 2) * LANES : (extent + 3) * LANES, :] = blank
        for t in range(tools):
            band_fwd[t, (extent + 1) * LANES : (extent + 2) * LANES, :] = blank

        def toeplitz(head, shift, which):
            square = jnp.broadcast_to(head, (LANES, LANES))
            turned = pltpu.roll(square, shift, axis=1, stride=1, stride_axis=0)
            return (turned * keep[which]).astype(BF16)

        @pl.loop(0, extent, unroll=4)
        def _(i):
            at_i = pl.ds(pl.multiple_of((extent + 1 - i) * LANES, LANES), LANES)
            band_adj[at_i, :] = toeplitz(head_adj[pl.ds(i, 1), :], extent, 0)

        k_of = lax.broadcasted_iota(jnp.int32, (words, LANES), 0)
        b_of = lax.broadcasted_iota(jnp.int32, (words, LANES), 1)
        bits_copy.wait()
        word = bits_ref[...].reshape(tools * rows, words)
        low_byte = (word & 255).astype(F32).astype(BF16)
        high_byte = (word >> 8).astype(F32).astype(BF16)
        for c in range(tiles):
            mine = k_of == c * (LANES // 16) + b_of // 16
            upper = b_of % 16 >= 8
            byte = jnp.dot(low_byte, (mine & ~upper).astype(BF16), preferred_element_type=F32)
            byte += jnp.dot(high_byte, (mine & upper).astype(BF16), preferred_element_type=F32)
            bit_at = lax.broadcasted_iota(jnp.int32, byte.shape, 1) % 8
            allowed[pl.ds(c, tools * rows, stride=tiles), :] = (
                (byte.astype(jnp.int32) >> bit_at) & 1
            ).astype(F32)

        def assemble(target, d, two_rows):
            @pl.loop(0, pairs, unroll=4)
            def _(m):
                both = two_rows(m)
                for a in range(2):
                    row = both[a * tiles : (a + 1) * tiles]
                    before = jnp.broadcast_to(edge[0, pl.ds(2 * m + a, 1), :], (SUB, LANES))
                    after = jnp.broadcast_to(edge[1, pl.ds(2 * m + a, 1), :], (SUB, LANES))
                    prior = jnp.where(sub == 0, before, pltpu.roll(row, 1, axis=0))
                    later = jnp.where(sub == SUB - 1, after, pltpu.roll(row, SUB - 1, axis=0))
                    even = pltpu.roll(jnp.where(lane >= 96, prior, row), 32, axis=1)
                    odd = pltpu.roll(jnp.where(lane < 32, later, row), 96, axis=1)
                    target[
                        pl.ds(pl.multiple_of((pairs * d + m) * 16, 16), 16),
                        a * LANES : (a + 1) * LANES,
                    ] = jnp.concatenate([even, odd], axis=0).astype(BF16)

        def at_pair(m):
            return pl.ds(pl.multiple_of(m * 2 * tiles, 2 * tiles), 2 * tiles)

        def fill_blank(target, d):
            target[d * pairs * 16 : (d + 1) * pairs * 16, :] = jnp.zeros((pairs * 16, 2 * LANES), BF16)

        def over_blocks(block, blank_of=None):
            block(1)
            for d, there in ((0, has_up), (2, has_down)):
                pl.when(there)(lambda d=d: block(d))
                if blank_of is not None:
                    pl.when(jnp.logical_not(there))(lambda d=d: blank_of(d))

        def adjoint(out):
            acc[...] = jnp.zeros_like(acc)

            @pl.loop(0, steps // 3)
            def _(kk):
                lhs = jnp.concatenate(
                    [
                        win_adj[pl.ds(pl.multiple_of((3 * kk + u) * 16, 16), pairs * 16), :]
                        for u in range(3)
                    ],
                    axis=1,
                )
                first = pl.multiple_of(6 * kk * LANES, LANES)
                rhs = jnp.concatenate(
                    [
                        band_adj[pl.ds(first + LANES, 6 * LANES), :],
                        band_adj[pl.ds(first, 6 * LANES), :],
                    ],
                    axis=1,
                )
                acc[...] += jnp.dot(lhs, rhs, preferred_element_type=F32)

            def finish(m, total):
                for b in range(2):
                    cols = slice(b * LANES, (b + 1) * LANES)
                    even = acc[pl.ds(pl.multiple_of(m * 16, 16), 8), cols]
                    odd = acc[pl.ds(pl.multiple_of(m * 16 + 8, 8), 8), cols]
                    values = (
                        jnp.where(left_half, even, pltpu.roll(odd, 64, axis=1)),
                        jnp.where(left_half, pltpu.roll(even, 64, axis=1), odd),
                    )
                    for t in range(tools):
                        at_r = pl.ds(pl.multiple_of((t * rows + 2 * m + b) * tiles, tiles), tiles)
                        value = allowed[at_r, :] * values[t]
                        out[at_r, :] = value
                        total = total + value * value
                return total

            return lax.fori_loop(0, pairs, finish, jnp.zeros((SUB, LANES), F32), unroll=4)

        def sum_stage(which, source, box, count, peer_of):
            def copy_to(step):
                return pltpu.make_async_remote_copy(
                    src_ref=msg.at[source],
                    dst_ref=box.at[step - 1],
                    send_sem=sum_send.at[which],
                    recv_sem=sum_recv.at[which],
                    device_id=peer_of(step),
                    device_id_type=MESH,
                )

            for step in range(1, count):
                copy_to(step).start()

            all_of = pltpu.make_async_remote_copy(
                src_ref=box,
                dst_ref=box,
                send_sem=sum_send.at[which],
                recv_sem=sum_recv.at[which],
                device_id=peer_of(1),
                device_id_type=MESH,
            )
            return all_of

        def total_of(first, side_work):
            stage = sum_stage(first, first, box_a.at[first // 2], plane_count, plane_peer)
            side_work()
            stage.wait_recv()
            msg[first + 1] = msg[first] + jnp.sum(box_a[first // 2], axis=0)
            other = sum_stage(first + 1, first + 1, box_b.at[first // 2], line_count, line_peer)
            other.wait_recv()
            everything = msg[first + 1] + jnp.sum(box_b[first // 2], axis=0)
            return jnp.sum(everything, axis=1, keepdims=True), (stage, other)

        first_halo[1]()

        def first_block(d):
            if d == 1:
                edge[...] = low_edge_in[1].astype(F32)
                assemble(win_adj, 1, lambda m: masked[1, at_pair(m), :])
            else:
                edge[...] = low_edge_in[d].astype(F32)
                assemble(win_adj, d, lambda m: low_in[d, at_pair(m), :].astype(F32))

        over_blocks(first_block, lambda d: fill_blank(win_adj, d))
        masked_halo[0]()
        gamma_part = adjoint(gradient)
        grad_low[...] = gradient[...].astype(BF16)
        for side, tile in ((0, tiles - 1), (1, 0)):
            grad_edge_out[side] = gradient[pl.ds(tile, tools * rows, stride=tiles), :].astype(BF16)
        grad_halo[0]()

        for t in range(tools):

            @pl.loop(0, extent + 1, unroll=5)
            def _(q, t=t):
                at_q = pl.ds(pl.multiple_of(q * LANES, LANES), LANES)
                band_fwd[t, at_q, :] = toeplitz(head_fwd[t, pl.ds(q, 1), :], extent + 1, 1)

        grad_halo[1]()

        def grad_block(d):
            for t in range(tools):
                edge[...] = grad_edge_in[d, :, t * rows : (t + 1) * rows, :].astype(F32)
                first = t * field
                if d == 1:
                    assemble(win_fwd.at[t], 1, lambda m, first=first: gradient[pl.ds(pl.multiple_of(first + m * 16, 16), 16), :])
                else:
                    assemble(
                        win_fwd.at[t],
                        d,
                        lambda m, first=first: grad_in[
                            d, pl.ds(pl.multiple_of(first + m * 16, 16), 16), :
                        ].astype(F32),
                    )

        def grad_blank(d):
            for t in range(tools):
                fill_blank(win_fwd.at[t], d)

        over_blocks(grad_block, grad_blank)

        acc_fwd[...] = jnp.zeros_like(acc_fwd)

        @pl.loop(0, steps // 3)
        def _(kk):
            lhs = jnp.concatenate(
                [
                    win_fwd[t, pl.ds(pl.multiple_of((3 * kk + u) * 16, 16), pairs * 16), :]
                    for t in range(tools)
                    for u in range(3)
                ],
                axis=1,
            )
            first = pl.multiple_of(6 * kk * LANES, LANES)
            rhs = jnp.concatenate(
                [band_fwd[t, pl.ds(first, 6 * LANES), :] for t in range(tools)], axis=0
            )
            acc_fwd[...] += jnp.dot(lhs, rhs, preferred_element_type=F32)

        @pl.loop(0, pairs, unroll=4)
        def _(m):
            even = acc_fwd[pl.ds(pl.multiple_of(m * 16, 16), 8), :]
            odd = acc_fwd[pl.ds(pl.multiple_of(m * 16 + 8, 8), 8), :]
            top = jnp.where(left_half, even, pltpu.roll(odd, 64, axis=1))
            low = jnp.where(left_half, pltpu.roll(even, 64, axis=1), odd)
            at_m = at_pair(m)
            part[at_m, :] = inside[at_m, :] * jnp.concatenate([top, low], axis=0)

        tool_copies = []
        for step in range(1, tool_count):
            tool_copies.append(
                pltpu.make_async_remote_copy(
                    src_ref=part,
                    dst_ref=part_in.at[step - 1],
                    send_sem=tool_sem.at[0, step - 1],
                    recv_sem=tool_sem.at[1, step - 1],
                    device_id={"az": az, "rad": rad, "tool": lax.rem(tool + step, tool_count)},
                    device_id_type=MESH,
                )
            )
        for copy in tool_copies:
            copy.start()
        for copy in tool_copies:
            copy.wait_recv()

        def join(m, total):
            at_m = at_pair(m)
            value = part[at_m, :]
            for step in range(1, tool_count):
                value = value + part_in[step - 1, at_m, :]
            removal[1, at_m, :] = value
            return total + value[:SUB] * value[:SUB] + value[SUB:] * value[SUB:]

        curvature_part = lax.fori_loop(0, pairs, join, jnp.zeros((SUB, LANES), F32), unroll=4)
        for side, tile in ((0, tiles - 1), (1, 0)):
            removal_edge_out[side] = removal[1, pl.ds(tile, rows, stride=tiles), :]
        msg[0] = jnp.concatenate(
            [
                jnp.sum(gamma_part, axis=0, keepdims=True),
                jnp.sum(curvature_part, axis=0, keepdims=True),
            ],
            axis=0,
        )

        def beside():
            removal_halo[0]()
            masked_halo[1]()
            removal_halo[1]()
            dwell_copy.wait()

        sums, stages = total_of(0, beside)
        gamma = sums[0:1]
        curvature = sums[1:2] * (1.0 / tool_count)
        step_size = gamma / (curvature + EPSILON)

        def second_block(d):
            edge[...] = masked_edge[d] - step_size * removal_edge[d]
            assemble(
                win_adj, d, lambda m: masked[d, at_pair(m), :] - step_size * removal[d, at_pair(m), :]
            )

        over_blocks(second_block)
        new_part = adjoint(gradient_new)
        new_row = jnp.sum(new_part, axis=0, keepdims=True)
        msg[2] = jnp.concatenate([new_row, new_row], axis=0)

        dwell_store = pltpu.make_async_copy(dwell_res, dwell_out, local_sem.at[2])
        residual_store = pltpu.make_async_copy(residual_res, residual_out, local_sem.at[3])
        direction_store = pltpu.make_async_copy(direction_res, direction_out, local_sem.at[4])

        def outputs():
            for t in range(tools):
                for c in range(tiles):
                    cols = slice(c * LANES, (c + 1) * LANES)
                    step_of = gradient[pl.ds(t * field + c, rows, stride=tiles), :]
                    dwell_res[t, :, cols] = dwell_v[t, :, cols] + step_size * step_of
            dwell_store.start()
            for c in range(share_tiles):
                from_c = pl.ds(tool * share_tiles + c, rows, stride=tiles)
                residual_res[:, c * LANES : (c + 1) * LANES] = (
                    whole[from_c, :] - step_size * removal[1, from_c, :]
                )
            residual_store.start()

        new_sums, new_stages = total_of(2, outputs)
        ratio = new_sums[0:1] / (gamma + EPSILON)
        for t in range(tools):
            for c in range(tiles):
                cols = slice(c * LANES, (c + 1) * LANES)
                from_c = pl.ds(t * field + c, rows, stride=tiles)
                direction_res[t, :, cols] = gradient_new[from_c, :] + ratio * gradient[from_c, :]
        direction_store.start()

        for phase in (first_halo, masked_halo, grad_halo, removal_halo):
            phase[2]()
        for copy in tool_copies:
            copy.wait_send()
        for stage in stages + new_stages:
            stage.wait_send()
        dwell_store.wait()
        residual_store.wait()
        direction_store.wait()

    hbm_spec = pl.BlockSpec(memory_space=pltpu.HBM)
    scratch = [
        ((rows, width), F32),
        (dwell_shape, F32),
        ((field, LANES), F32),
        ((3, field, LANES), F32),
        ((3, 2, rows, LANES), F32),
        ((2, rows, LANES), F32),
        ((field, LANES), BF16),
        ((2, rows, LANES), BF16),
        ((3, field, LANES), BF16),
        ((3, 2, rows, LANES), BF16),
        ((field, LANES), F32),
        ((tools * field, LANES), F32),
        ((extent, LANES), F32),
        ((tools, extent + 8, LANES), F32),
        ((tools, extent + 8, LANES), F32),
        ((2, LANES, LANES), F32),
        (((extent + 3) * LANES, LANES), BF16),
        ((tools, (extent + 2) * LANES, LANES), BF16),
        ((3 * pairs * 16, 2 * LANES), BF16),
        ((tools, 3 * pairs * 16, 2 * LANES), BF16),
        ((pairs * 16, 2 * LANES), F32),
        ((pairs * 16, LANES), F32),
        ((tools * field, LANES), F32),
        ((tools * field, LANES), BF16),
        ((2, tools * rows, LANES), BF16),
        ((3, tools * field, LANES), BF16),
        ((3, 2, tools * rows, LANES), BF16),
        ((field, LANES), F32),
        ((tool_count - 1, field, LANES), F32),
        ((3, field, LANES), F32),
        ((2, rows, LANES), F32),
        ((3, 2, rows, LANES), F32),
        ((2, rows, LANES), F32),
        ((tools * field, LANES), F32),
        (dwell_shape, F32),
        ((rows, share), F32),
        (dwell_shape, F32),
        ((4, 2, LANES), F32),
        ((2, plane_count - 1, 2, LANES), F32),
        ((2, line_count - 1, 2, LANES), F32),
    ]
    return pl.pallas_call(
        body,
        out_shape=(
            jax.ShapeDtypeStruct(dwell_shape, F32),
            jax.ShapeDtypeStruct((rows, share), F32),
            jax.ShapeDtypeStruct(dwell_shape, F32),
        ),
        in_specs=[hbm_spec] * 6,
        out_specs=(hbm_spec,) * 3,
        scratch_shapes=[
            pltpu.VMEM(influence_shape, BF16),
            pltpu.SMEM((rows,), jnp.int32),
            pltpu.SMEM((rows,), jnp.int32),
            pltpu.VMEM((tools, rows, words), jnp.int32),
        ]
        + [pltpu.VMEM(shape, dtype) for shape, dtype in scratch]
        + [
            pltpu.SemaphoreType.DMA((9,)),
            pltpu.SemaphoreType.DMA((4, 9)),
            pltpu.SemaphoreType.DMA((4, 9)),
            pltpu.SemaphoreType.DMA((2, max(tool_count - 1, 1))),
            pltpu.SemaphoreType.DMA((4,)),
            pltpu.SemaphoreType.DMA((4,)),
        ],
        compiler_params=pltpu.CompilerParams(
            collective_id=0, has_side_effects=True, vmem_limit_bytes=24 * 1024 * 1024
        ),
        name="cgls",
    )


def hand_on(results):
    count = len(results)

    def body(*refs):
        sem = refs[-1]
        copies = [
            pltpu.make_async_copy(refs[i], refs[count + i], sem.at[i]) for i in range(count)
        ]
        for copy in copies:
            copy.start()
        for copy in copies:
            copy.wait()

    return pl.pallas_call(
        body,
        out_shape=tuple(jax.ShapeDtypeStruct(x.shape, x.dtype) for x in results),
        in_specs=[pl.BlockSpec(memory_space=pl.ANY)] * count,
        out_specs=(pl.BlockSpec(memory_space=pltpu.HBM),) * count,
        scratch_shapes=[pltpu.SemaphoreType.DMA((count,))],
        name="hand_on",
    )(*(pltpu.with_memory_space_constraint(x, pltpu.VMEM) for x in results))


def solution(mesh):
    def per_device(dwell, residual, influence, cycle_start, cycle_end, allowed_bits):
        call = build(
            dwell.shape,
            influence.shape,
            allowed_bits.shape[-1],
            mesh.shape["az"],
            mesh.shape["rad"],
            mesh.shape["tool"],
        )
        given = (dwell, residual, influence, cycle_start, cycle_end, allowed_bits)
        return hand_on(call(*(pltpu.with_memory_space_constraint(x, pltpu.HBM) for x in given)))

    in_specs = (
        P("tool", "rad", "az"),
        P("rad", "az"),
        P("tool", None, None),
        P("rad"),
        P("rad"),
        P("tool", "rad", "az"),
    )
    out_specs = (P("tool", "rad", "az"), P("rad", ("az", "tool")), P("tool", "rad", "az"))
    return jax.shard_map(
        per_device, mesh=mesh, in_specs=in_specs, out_specs=out_specs, check_vma=False
    )
```

```python
import jax
import jax.numpy as jnp
from jax import lax
from jax.experimental import pallas as pl
from jax.experimental.pallas import tpu as pltpu
from jax.sharding import PartitionSpec as P

EPSILON = 1e-06
MESH = pl.DeviceIdType.MESH
F32 = jnp.float32
BF16 = jnp.bfloat16
LANES = 128
SUB = 8


def meetings_of(line_count):
    return max(line_count // 2, 1).bit_length() - 1


def build(dwell_shape, influence_shape, words, az_count, rad_count, tool_count):
    tools, rows, width = dwell_shape
    extent = influence_shape[-1]
    tiles = width // LANES
    assert tiles == SUB and extent == 64 and rows == 32
    pairs = rows // 2
    field = rows * tiles
    steps = extent // 2 + 1
    group = 11
    assert steps % group == 0
    plane_count = 2 * rad_count * tool_count
    line_count = az_count // 2
    for count in (az_count, rad_count, tool_count):
        assert count & (count - 1) == 0
    share = width // tool_count
    share_tiles = share // LANES

    def body(
        dwell_hbm,
        residual_hbm,
        influence_hbm,
        start_hbm,
        end_hbm,
        bits_hbm,
        dwell_out,
        residual_out,
        direction_out,
        influence_ref,
        start_ref,
        end_ref,
        bits_ref,
        natural,
        dwell_v,
        whole,
        masked,
        masked_edge,
        masked_edge_out,
        low_out,
        low_edge_out,
        low_in,
        low_edge_in,
        inside,
        allowed,
        head_adj,
        head_fwd,
        head_two,
        keep,
        band_adj,
        band_fwd,
        win_adj,
        win_fwd,
        acc,
        acc_fwd,
        gradient,
        grad_low,
        grad_edge_out,
        grad_in,
        grad_edge_in,
        part,
        part_in,
        removal,
        removal_edge_out,
        removal_edge,
        edge,
        gradient_new,
        msg,
        box_a,
        box_b,
        local_sem,
        halo_send,
        halo_recv,
        tool_sem,
        meet,
        sum_send,
        sum_recv,
    ):
        az, rad, tool = lax.axis_index("az"), lax.axis_index("rad"), lax.axis_index("tool")
        lane = lax.broadcasted_iota(jnp.int32, (SUB, LANES), 1)
        sub = lax.broadcasted_iota(jnp.int32, (SUB, LANES), 0)
        left_half = lane < LANES // 2

        residual_copy = pltpu.make_async_copy(residual_hbm, natural, local_sem.at[0])
        start_copy = pltpu.make_async_copy(start_hbm, start_ref, local_sem.at[5])
        end_copy = pltpu.make_async_copy(end_hbm, end_ref, local_sem.at[6])
        influence_copy = pltpu.make_async_copy(influence_hbm, influence_ref, local_sem.at[7])
        bits_copy = pltpu.make_async_copy(bits_hbm, bits_ref, local_sem.at[8])
        dwell_copy = pltpu.make_async_copy(dwell_hbm, dwell_v, local_sem.at[1])
        for copy in (residual_copy, start_copy, end_copy, influence_copy, bits_copy, dwell_copy):
            copy.start()

        def at(dr, da):
            return {
                "az": lax.rem(az + da + az_count, az_count),
                "rad": rad + dr,
                "tool": tool,
            }

        def plane_peer(step):
            return {
                "az": az ^ (step % 2),
                "rad": rad ^ (step // (2 * tool_count)),
                "tool": tool ^ (step // 2 % tool_count),
            }

        def line_peer(step):
            return {"az": az ^ (2 * step), "rad": rad, "tool": tool}

        has_up, has_down = rad > 0, rad < rad_count - 1

        barrier = pltpu.get_barrier_semaphore()

        def greet(peer):
            pl.semaphore_signal(barrier, inc=1, device_id=peer, device_id_type=MESH)

        for step in range(1, plane_count):
            greet(plane_peer(step))
        outer = 1 - 2 * (1 - lax.rem(az, 2))
        greet(at(0, outer))
        greet(at(0, 2))
        greet(at(0, -2))

        @pl.when(has_up)
        def _():
            greet(at(-1, outer))

        @pl.when(has_down)
        def _():
            greet(at(1, outer))

        residual_copy.wait()
        for c in range(tiles):
            whole[pl.ds(c, rows, stride=tiles), :] = natural[:, c * LANES : (c + 1) * LANES]
        start_copy.wait()
        end_copy.wait()
        column = az * width + sub * LANES + lane

        @pl.loop(0, rows, unroll=4)
        def _(r):
            at_r = pl.ds(pl.multiple_of(r * tiles, tiles), tiles)
            valid = ((column >= start_ref[r]) & (column < end_ref[r])).astype(F32)
            inside[at_r, :] = valid
            masked[1, at_r, :] = valid * whole[at_r, :]

        low_out[...] = masked[1].astype(BF16)
        for side, tile in ((0, tiles - 1), (1, 0)):
            tile_of = masked[1, pl.ds(tile, rows, stride=tiles), :]
            masked_edge_out[side] = tile_of
            low_edge_out[side] = tile_of.astype(BF16)

        extra = 1 + has_up.astype(jnp.int32) + has_down.astype(jnp.int32)
        pl.semaphore_wait(barrier, plane_count + 1 + extra)

        meetings = meetings_of(line_count)

        def meet_send(step):
            if step < meetings:
                for da in (2 << step, -(2 << step)):
                    pl.semaphore_signal(meet.at[step], inc=1, device_id=at(0, da), device_id_type=MESH)

        def meet_wait(step):
            if step < meetings:
                pl.semaphore_wait(meet.at[step], 2)

        def meet_last():
            for step in range(2, meetings):
                if step > 2:
                    meet_send(step)
                meet_wait(step)

        def halo(phase, mid_src, mid_dst, edge_src, edge_dst):
            copies = []
            for d in (0, 2, 1):
                for side, da in ((1, 0), (0, 1), (2, -1)):
                    if d == 1 and side == 1:
                        continue
                    src = mid_src if side == 1 else edge_src.at[side // 2]
                    dst = mid_dst.at[d] if side == 1 else edge_dst.at[d, side // 2]
                    copy = pltpu.make_async_remote_copy(
                        src_ref=src,
                        dst_ref=dst,
                        send_sem=halo_send.at[phase, 3 * d + side],
                        recv_sem=halo_recv.at[phase, 3 * d + side],
                        device_id=at(1 - d, da),
                        device_id_type=MESH,
                    )
                    copies.append((d, copy))

            def start():
                for d, copy in copies:
                    if d == 1:
                        copy.start()
                    else:
                        pl.when(has_down if d == 0 else has_up)(copy.start)

            def wait_recv(block):
                for d, copy in copies:
                    if d == block:
                        copy.wait_recv()

            def wait_send():
                for d, copy in copies:
                    if d == 1:
                        copy.wait_send()
                    else:
                        pl.when(has_down if d == 0 else has_up)(copy.wait_send)

            return start, wait_recv, wait_send

        first_halo = halo(0, low_out, low_in, low_edge_out, low_edge_in)
        masked_halo = halo(1, masked.at[1], masked, masked_edge_out, masked_edge)
        grad_halo = halo(2, grad_low, grad_in, grad_edge_out, grad_edge_in)
        removal_halo = halo(3, removal.at[1], removal, removal_edge_out, removal_edge)

        first_halo[0]()
        meet_send(0)

        influence_copy.wait()
        j_of = lax.broadcasted_iota(jnp.int32, (extent, LANES), 0)
        l_of = lax.broadcasted_iota(jnp.int32, (extent, LANES), 1)

        def spread(rows_of, where_j):
            return jnp.dot(rows_of, (l_of == where_j).astype(BF16), preferred_element_type=F32)

        head_adj[...] = spread(influence_ref[0], j_of) + spread(influence_ref[1], extent + j_of)
        head_fwd[...] = jnp.zeros_like(head_fwd)
        head_two[...] = jnp.zeros_like(head_two)
        for t in range(tools):
            head_fwd[t, 0:extent, :] = spread(influence_ref[t], extent - 1 - j_of)
            head_two[t, 1 : extent + 1, :] = spread(influence_ref[t], 2 * extent - 1 - j_of)
        head_fwd[...] = head_fwd[...] + head_two[...]
        c_of = lax.broadcasted_iota(jnp.int32, (LANES, LANES), 0)
        o_of = lax.broadcasted_iota(jnp.int32, (LANES, LANES), 1)
        low_side = o_of < extent
        off = o_of - c_of
        adj_keep = (low_side & (off >= -extent) & (off < 0)) | (~low_side & (off >= 0) & (off < extent))
        fwd_keep = (low_side & (off > -extent) & (off <= 0)) | (~low_side & (off > 0) & (off <= extent))
        keep[0] = adj_keep.astype(F32)
        keep[1] = fwd_keep.astype(F32)
        blank = jnp.zeros((LANES, LANES), BF16)
        band_adj[0:LANES, :] = blank
        band_adj[LANES : 2 * LANES, :] = blank
        band_adj[(extent + 2) * LANES : (extent + 3) * LANES, :] = blank
        for t in range(tools):
            band_fwd[t, (extent + 1) * LANES : (extent + 2) * LANES, :] = blank

        def toeplitz(head, shift, which):
            square = jnp.broadcast_to(head, (LANES, LANES))
            turned = pltpu.roll(square, shift, axis=1, stride=1, stride_axis=0)
            return (turned * keep[which]).astype(BF16)

        @pl.loop(0, extent, unroll=4)
        def _(i):
            at_i = pl.ds(pl.multiple_of((extent + 1 - i) * LANES, LANES), LANES)
            band_adj[at_i, :] = toeplitz(head_adj[pl.ds(i, 1), :], extent, 0)

        k_of = lax.broadcasted_iota(jnp.int32, (words, LANES), 0)
        b_of = lax.broadcasted_iota(jnp.int32, (words, LANES), 1)
        bits_copy.wait()
        word = bits_ref[...].reshape(tools * rows, words)
        low_byte = (word & 255).astype(F32).astype(BF16)
        high_byte = (word >> 8).astype(F32).astype(BF16)
        for c in range(tiles):
            mine = k_of == c * (LANES // 16) + b_of // 16
            upper = b_of % 16 >= 8
            byte = jnp.dot(low_byte, (mine & ~upper).astype(BF16), preferred_element_type=F32)
            byte += jnp.dot(high_byte, (mine & upper).astype(BF16), preferred_element_type=F32)
            bit_at = lax.broadcasted_iota(jnp.int32, byte.shape, 1) % 8
            allowed[pl.ds(c, tools * rows, stride=tiles), :] = (
                (byte.astype(jnp.int32) >> bit_at) & 1
            ).astype(F32)

        def assemble(target, d, two_rows):
            @pl.loop(0, pairs, unroll=4)
            def _(m):
                both = two_rows(m)
                for a in range(2):
                    row = both[a * tiles : (a + 1) * tiles]
                    before = jnp.broadcast_to(edge[0, pl.ds(2 * m + a, 1), :], (SUB, LANES))
                    after = jnp.broadcast_to(edge[1, pl.ds(2 * m + a, 1), :], (SUB, LANES))
                    prior = jnp.where(sub == 0, before, pltpu.roll(row, 1, axis=0))
                    later = jnp.where(sub == SUB - 1, after, pltpu.roll(row, SUB - 1, axis=0))
                    even = pltpu.roll(jnp.where(lane >= 96, prior, row), 32, axis=1)
                    odd = pltpu.roll(jnp.where(lane < 32, later, row), 96, axis=1)
                    target[
                        pl.ds(pl.multiple_of((pairs * d + m) * 16, 16), 16),
                        a * LANES : (a + 1) * LANES,
                    ] = jnp.concatenate([even, odd], axis=0).astype(BF16)

        def at_pair(m):
            return pl.ds(pl.multiple_of(m * 2 * tiles, 2 * tiles), 2 * tiles)

        def fill_blank(target, d):
            target[d * pairs * 16 : (d + 1) * pairs * 16, :] = jnp.zeros((pairs * 16, 2 * LANES), BF16)

        def over_blocks(block, blank_of=None):
            block(1)
            for d, there in ((0, has_up), (2, has_down)):
                pl.when(there)(lambda d=d: block(d))
                if blank_of is not None:
                    pl.when(jnp.logical_not(there))(lambda d=d: blank_of(d))

        def adjoint(out):
            acc[...] = jnp.zeros_like(acc)

            @pl.loop(0, steps // group)
            def _(kk):
                lhs = jnp.concatenate(
                    [
                        win_adj[pl.ds(pl.multiple_of((group * kk + u) * 16, 16), pairs * 16), :]
                        for u in range(group)
                    ],
                    axis=1,
                )
                first = pl.multiple_of(2 * group * kk * LANES, LANES)
                rhs = jnp.concatenate(
                    [
                        band_adj[pl.ds(first + LANES, 2 * group * LANES), :],
                        band_adj[pl.ds(first, 2 * group * LANES), :],
                    ],
                    axis=1,
                )
                acc[...] += jnp.dot(lhs, rhs, preferred_element_type=F32)

            def finish(m, total):
                for b in range(2):
                    cols = slice(b * LANES, (b + 1) * LANES)
                    even = acc[pl.ds(pl.multiple_of(m * 16, 16), 8), cols]
                    odd = acc[pl.ds(pl.multiple_of(m * 16 + 8, 8), 8), cols]
                    values = (
                        jnp.where(left_half, even, pltpu.roll(odd, 64, axis=1)),
                        jnp.where(left_half, pltpu.roll(even, 64, axis=1), odd),
                    )
                    for t in range(tools):
                        at_r = pl.ds(pl.multiple_of((t * rows + 2 * m + b) * tiles, tiles), tiles)
                        value = allowed[at_r, :] * values[t]
                        out[at_r, :] = value
                        total = total + value * value
                return total

            return lax.fori_loop(0, pairs, finish, jnp.zeros((SUB, LANES), F32), unroll=4)

        def sum_stage(which, source, box, count, peer_of):
            def copy_to(step):
                return pltpu.make_async_remote_copy(
                    src_ref=msg.at[source],
                    dst_ref=box.at[step - 1],
                    send_sem=sum_send.at[which],
                    recv_sem=sum_recv.at[which],
                    device_id=peer_of(step),
                    device_id_type=MESH,
                )

            for step in range(1, count):
                copy_to(step).start()

            all_of = pltpu.make_async_remote_copy(
                src_ref=box,
                dst_ref=box,
                send_sem=sum_send.at[which],
                recv_sem=sum_recv.at[which],
                device_id=peer_of(1),
                device_id_type=MESH,
            )
            return all_of

        def total_of(first, beside_plane, beside_line):
            stage = sum_stage(first, first, box_a.at[first // 2], plane_count, plane_peer)
            beside_plane()
            stage.wait_recv()
            msg[first + 1] = msg[first] + jnp.sum(box_a[first // 2], axis=0)
            other = sum_stage(first + 1, first + 1, box_b.at[first // 2], line_count, line_peer)
            beside_line()
            other.wait_recv()
            everything = msg[first + 1] + jnp.sum(box_b[first // 2], axis=0)
            return jnp.sum(everything, axis=1, keepdims=True), (stage, other)

        def first_block(d):
            first_halo[1](d)
            if d == 1:
                edge[...] = low_edge_in[1].astype(F32)
                assemble(win_adj, 1, lambda m: masked[1, at_pair(m), :])
            else:
                edge[...] = low_edge_in[d].astype(F32)
                assemble(win_adj, d, lambda m: low_in[d, at_pair(m), :].astype(F32))

        over_blocks(first_block, lambda d: fill_blank(win_adj, d))
        masked_halo[0]()
        gamma_part = adjoint(gradient)
        grad_low[...] = gradient[...].astype(BF16)
        for side, tile in ((0, tiles - 1), (1, 0)):
            grad_edge_out[side] = gradient[pl.ds(tile, tools * rows, stride=tiles), :].astype(BF16)
        grad_halo[0]()
        meet_wait(0)
        meet_send(1)

        for t in range(tools):

            @pl.loop(0, extent + 1, unroll=5)
            def _(q, t=t):
                at_q = pl.ds(pl.multiple_of(q * LANES, LANES), LANES)
                band_fwd[t, at_q, :] = toeplitz(head_fwd[t, pl.ds(q, 1), :], extent + 1, 1)

        def grad_block(d):
            grad_halo[1](d)
            for t in range(tools):
                edge[...] = grad_edge_in[d, :, t * rows : (t + 1) * rows, :].astype(F32)
                first = t * field
                if d == 1:
                    assemble(win_fwd.at[t], 1, lambda m, first=first: gradient[pl.ds(pl.multiple_of(first + m * 16, 16), 16), :])
                else:
                    assemble(
                        win_fwd.at[t],
                        d,
                        lambda m, first=first: grad_in[
                            d, pl.ds(pl.multiple_of(first + m * 16, 16), 16), :
                        ].astype(F32),
                    )

        def grad_blank(d):
            for t in range(tools):
                fill_blank(win_fwd.at[t], d)

        over_blocks(grad_block, grad_blank)

        acc_fwd[...] = jnp.zeros_like(acc_fwd)

        @pl.loop(0, steps // group)
        def _(kk):
            lhs = jnp.concatenate(
                [
                    win_fwd[t, pl.ds(pl.multiple_of((group * kk + u) * 16, 16), pairs * 16), :]
                    for t in range(tools)
                    for u in range(group)
                ],
                axis=1,
            )
            first = pl.multiple_of(2 * group * kk * LANES, LANES)
            rhs = jnp.concatenate(
                [band_fwd[t, pl.ds(first, 2 * group * LANES), :] for t in range(tools)], axis=0
            )
            acc_fwd[...] += jnp.dot(lhs, rhs, preferred_element_type=F32)

        @pl.loop(0, pairs, unroll=4)
        def _(m):
            even = acc_fwd[pl.ds(pl.multiple_of(m * 16, 16), 8), :]
            odd = acc_fwd[pl.ds(pl.multiple_of(m * 16 + 8, 8), 8), :]
            top = jnp.where(left_half, even, pltpu.roll(odd, 64, axis=1))
            low = jnp.where(left_half, pltpu.roll(even, 64, axis=1), odd)
            at_m = at_pair(m)
            part[at_m, :] = inside[at_m, :] * jnp.concatenate([top, low], axis=0)

        tool_copies = []
        for step in range(1, tool_count):
            tool_copies.append(
                pltpu.make_async_remote_copy(
                    src_ref=part,
                    dst_ref=part_in.at[step - 1],
                    send_sem=tool_sem.at[0, step - 1],
                    recv_sem=tool_sem.at[1, step - 1],
                    device_id={"az": az, "rad": rad, "tool": lax.rem(tool + step, tool_count)},
                    device_id_type=MESH,
                )
            )
        for copy in tool_copies:
            copy.start()
        meet_wait(1)
        meet_send(2)
        for copy in tool_copies:
            copy.wait_recv()

        def join(m, total):
            at_m = at_pair(m)
            value = part[at_m, :]
            for step in range(1, tool_count):
                value = value + part_in[step - 1, at_m, :]
            removal[1, at_m, :] = value
            return total + value[:SUB] * value[:SUB] + value[SUB:] * value[SUB:]

        curvature_part = lax.fori_loop(0, pairs, join, jnp.zeros((SUB, LANES), F32), unroll=4)
        msg[0] = jnp.concatenate(
            [
                jnp.sum(gamma_part, axis=0, keepdims=True),
                jnp.sum(curvature_part, axis=0, keepdims=True),
            ],
            axis=0,
        )

        def edges():
            for side, tile in ((0, tiles - 1), (1, 0)):
                removal_edge_out[side] = removal[1, pl.ds(tile, rows, stride=tiles), :]
            dwell_copy.wait()
            meet_last()

        sums, stages = total_of(0, edges, removal_halo[0])
        gamma = sums[0:1]
        curvature = sums[1:2] * (1.0 / tool_count)
        step_size = gamma / (curvature + EPSILON)

        def second_block(d):
            masked_halo[1](d)
            removal_halo[1](d)
            edge[...] = masked_edge[d] - step_size * removal_edge[d]
            assemble(
                win_adj, d, lambda m: masked[d, at_pair(m), :] - step_size * removal[d, at_pair(m), :]
            )

        over_blocks(second_block)
        new_part = adjoint(gradient_new)
        new_row = jnp.sum(new_part, axis=0, keepdims=True)
        msg[2] = jnp.concatenate([new_row, new_row], axis=0)

        def dwell_output():
            for t in range(tools):
                for c in range(tiles):
                    cols = slice(c * LANES, (c + 1) * LANES)
                    step_of = gradient[pl.ds(t * field + c, rows, stride=tiles), :]
                    dwell_out[t, :, cols] = dwell_v[t, :, cols] + step_size * step_of

        def residual_output():
            for c in range(share_tiles):
                from_c = pl.ds(tool * share_tiles + c, rows, stride=tiles)
                residual_out[:, c * LANES : (c + 1) * LANES] = (
                    whole[from_c, :] - step_size * removal[1, from_c, :]
                )

        new_sums, new_stages = total_of(2, dwell_output, residual_output)
        ratio = new_sums[0:1] / (gamma + EPSILON)
        for t in range(tools):
            for c in range(tiles):
                cols = slice(c * LANES, (c + 1) * LANES)
                from_c = pl.ds(t * field + c, rows, stride=tiles)
                direction_out[t, :, cols] = gradient_new[from_c, :] + ratio * gradient[from_c, :]

        for phase in (first_halo, masked_halo, grad_halo, removal_halo):
            phase[2]()
        for copy in tool_copies:
            copy.wait_send()
        for stage in stages + new_stages:
            stage.wait_send()

    hbm_spec = pl.BlockSpec(memory_space=pltpu.HBM)
    scratch = [
        ((rows, width), F32),
        (dwell_shape, F32),
        ((field, LANES), F32),
        ((3, field, LANES), F32),
        ((3, 2, rows, LANES), F32),
        ((2, rows, LANES), F32),
        ((field, LANES), BF16),
        ((2, rows, LANES), BF16),
        ((3, field, LANES), BF16),
        ((3, 2, rows, LANES), BF16),
        ((field, LANES), F32),
        ((tools * field, LANES), F32),
        ((extent, LANES), F32),
        ((tools, extent + 8, LANES), F32),
        ((tools, extent + 8, LANES), F32),
        ((2, LANES, LANES), F32),
        (((extent + 3) * LANES, LANES), BF16),
        ((tools, (extent + 2) * LANES, LANES), BF16),
        ((3 * pairs * 16, 2 * LANES), BF16),
        ((tools, 3 * pairs * 16, 2 * LANES), BF16),
        ((pairs * 16, 2 * LANES), F32),
        ((pairs * 16, LANES), F32),
        ((tools * field, LANES), F32),
        ((tools * field, LANES), BF16),
        ((2, tools * rows, LANES), BF16),
        ((3, tools * field, LANES), BF16),
        ((3, 2, tools * rows, LANES), BF16),
        ((field, LANES), F32),
        ((tool_count - 1, field, LANES), F32),
        ((3, field, LANES), F32),
        ((2, rows, LANES), F32),
        ((3, 2, rows, LANES), F32),
        ((2, rows, LANES), F32),
        ((tools * field, LANES), F32),
        ((4, 2, LANES), F32),
        ((2, plane_count - 1, 2, LANES), F32),
        ((2, line_count - 1, 2, LANES), F32),
    ]
    return pl.pallas_call(
        body,
        out_shape=(
            pltpu.VMEM(dwell_shape, F32),
            pltpu.VMEM((rows, share), F32),
            pltpu.VMEM(dwell_shape, F32),
        ),
        in_specs=[hbm_spec] * 6,
        out_specs=(pl.BlockSpec(memory_space=pltpu.VMEM),) * 3,
        scratch_shapes=[
            pltpu.VMEM(influence_shape, BF16),
            pltpu.SMEM((rows,), jnp.int32),
            pltpu.SMEM((rows,), jnp.int32),
            pltpu.VMEM((tools, rows, words), jnp.int32),
        ]
        + [pltpu.VMEM(shape, dtype) for shape, dtype in scratch]
        + [
            pltpu.SemaphoreType.DMA((9,)),
            pltpu.SemaphoreType.DMA((4, 9)),
            pltpu.SemaphoreType.DMA((4, 9)),
            pltpu.SemaphoreType.DMA((2, max(tool_count - 1, 1))),
            pltpu.SemaphoreType.REGULAR((max(meetings_of(line_count), 1),)),
            pltpu.SemaphoreType.DMA((4,)),
            pltpu.SemaphoreType.DMA((4,)),
        ],
        compiler_params=pltpu.CompilerParams(
            collective_id=0, has_side_effects=True, vmem_limit_bytes=24 * 1024 * 1024
        ),
        name="cgls",
    )


def hand_on(results):
    count = len(results)

    def body(*refs):
        sem = refs[-1]
        copies = [
            pltpu.make_async_copy(refs[i], refs[count + i], sem.at[i]) for i in range(count)
        ]
        for copy in copies:
            copy.start()
        for copy in copies:
            copy.wait()

    return pl.pallas_call(
        body,
        out_shape=tuple(jax.ShapeDtypeStruct(x.shape, x.dtype) for x in results),
        in_specs=[pl.BlockSpec(memory_space=pl.ANY)] * count,
        out_specs=(pl.BlockSpec(memory_space=pltpu.HBM),) * count,
        scratch_shapes=[pltpu.SemaphoreType.DMA((count,))],
        name="hand_on",
    )(*(pltpu.with_memory_space_constraint(x, pltpu.VMEM) for x in results))


def solution(mesh):
    def per_device(dwell, residual, influence, cycle_start, cycle_end, allowed_bits):
        call = build(
            dwell.shape,
            influence.shape,
            allowed_bits.shape[-1],
            mesh.shape["az"],
            mesh.shape["rad"],
            mesh.shape["tool"],
        )
        given = (dwell, residual, influence, cycle_start, cycle_end, allowed_bits)
        return hand_on(call(*(pltpu.with_memory_space_constraint(x, pltpu.HBM) for x in given)))

    in_specs = (
        P("tool", "rad", "az"),
        P("rad", "az"),
        P("tool", None, None),
        P("rad"),
        P("rad"),
        P("tool", "rad", "az"),
    )
    out_specs = (P("tool", "rad", "az"), P("rad", ("az", "tool")), P("tool", "rad", "az"))
    return jax.shard_map(
        per_device, mesh=mesh, in_specs=in_specs, out_specs=out_specs, check_vma=False
    )
```

```python
import jax
import jax.numpy as jnp
from jax import lax
from jax.experimental import pallas as pl
from jax.experimental.pallas import tpu as pltpu
from jax.sharding import PartitionSpec as P

EPSILON = 1e-06
MESH = pl.DeviceIdType.MESH
F32 = jnp.float32
BF16 = jnp.bfloat16
LANES = 128
SUB = 8


def meetings_of(line_count):
    return max(line_count // 2, 1).bit_length() - 1


def build(dwell_shape, influence_shape, words, az_count, rad_count, tool_count):
    tools, rows, width = dwell_shape
    extent = influence_shape[-1]
    tiles = width // LANES
    assert tiles == SUB and extent == 64 and rows == 32
    pairs = rows // 2
    field = rows * tiles
    steps = extent // 2 + 1
    group = 11
    assert steps % group == 0
    plane_count = 2 * rad_count * tool_count
    line_count = az_count // 2
    for count in (az_count, rad_count, tool_count):
        assert count & (count - 1) == 0
    share = width // tool_count
    share_tiles = share // LANES

    def body(
        dwell_hbm,
        residual_hbm,
        influence_hbm,
        start_hbm,
        end_hbm,
        bits_hbm,
        dwell_out,
        residual_out,
        direction_out,
        influence_ref,
        start_ref,
        end_ref,
        bits_ref,
        natural,
        dwell_v,
        whole,
        masked,
        masked_edge,
        masked_edge_out,
        low_out,
        low_edge_out,
        low_in,
        low_edge_in,
        inside,
        allowed,
        head_adj,
        head_fwd,
        head_two,
        keep,
        band_adj,
        band_fwd,
        win_adj,
        win_fwd,
        acc,
        acc_fwd,
        gradient,
        grad_low,
        grad_edge_out,
        grad_in,
        grad_edge_in,
        part,
        part_in,
        removal,
        removal_edge_out,
        removal_edge,
        edge,
        gradient_new,
        grad_natural,
        msg,
        box_a,
        box_b,
        local_sem,
        halo_send,
        halo_recv,
        tool_sem,
        meet,
        sum_send,
        sum_recv,
    ):
        az, rad, tool = lax.axis_index("az"), lax.axis_index("rad"), lax.axis_index("tool")
        lane = lax.broadcasted_iota(jnp.int32, (SUB, LANES), 1)
        sub = lax.broadcasted_iota(jnp.int32, (SUB, LANES), 0)
        left_half = lane < LANES // 2

        residual_copy = pltpu.make_async_copy(residual_hbm, natural, local_sem.at[0])
        start_copy = pltpu.make_async_copy(start_hbm, start_ref, local_sem.at[5])
        end_copy = pltpu.make_async_copy(end_hbm, end_ref, local_sem.at[6])
        influence_copy = pltpu.make_async_copy(influence_hbm, influence_ref, local_sem.at[7])
        bits_copy = pltpu.make_async_copy(bits_hbm, bits_ref, local_sem.at[8])
        dwell_copy = pltpu.make_async_copy(dwell_hbm, dwell_v, local_sem.at[1])
        for copy in (residual_copy, start_copy, end_copy, influence_copy, bits_copy, dwell_copy):
            copy.start()

        def at(dr, da):
            return {
                "az": lax.rem(az + da + az_count, az_count),
                "rad": rad + dr,
                "tool": tool,
            }

        def plane_peer(step):
            return {
                "az": az ^ (step % 2),
                "rad": rad ^ (step // (2 * tool_count)),
                "tool": tool ^ (step // 2 % tool_count),
            }

        def line_peer(step):
            return {"az": az ^ (2 * step), "rad": rad, "tool": tool}

        has_up, has_down = rad > 0, rad < rad_count - 1

        barrier = pltpu.get_barrier_semaphore()

        def greet(peer):
            pl.semaphore_signal(barrier, inc=1, device_id=peer, device_id_type=MESH)

        outer = 1 - 2 * (1 - lax.rem(az, 2))
        greet(at(0, outer))
        greet(at(0, 2))
        greet(at(0, -2))

        @pl.when(has_up)
        def _():
            greet(at(-1, outer))

        @pl.when(has_down)
        def _():
            greet(at(1, outer))

        for step in range(1, plane_count):
            greet(plane_peer(step))

        residual_copy.wait()
        for c in range(tiles):
            whole[pl.ds(c, rows, stride=tiles), :] = natural[:, c * LANES : (c + 1) * LANES]
        start_copy.wait()
        end_copy.wait()
        column = az * width + sub * LANES + lane

        @pl.loop(0, rows, unroll=4)
        def _(r):
            at_r = pl.ds(pl.multiple_of(r * tiles, tiles), tiles)
            valid = ((column >= start_ref[r]) & (column < end_ref[r])).astype(F32)
            inside[at_r, :] = valid
            masked[1, at_r, :] = valid * whole[at_r, :]

        low_out[...] = masked[1].astype(BF16)
        for side, tile in ((0, tiles - 1), (1, 0)):
            tile_of = masked[1, pl.ds(tile, rows, stride=tiles), :]
            masked_edge_out[side] = tile_of
            low_edge_out[side] = tile_of.astype(BF16)

        extra = 1 + has_up.astype(jnp.int32) + has_down.astype(jnp.int32)
        pl.semaphore_wait(barrier, plane_count + 1 + extra)

        meetings = meetings_of(line_count)

        def meet_send(step):
            if step < meetings:
                for da in (2 << step, -(2 << step)):
                    pl.semaphore_signal(meet.at[step], inc=1, device_id=at(0, da), device_id_type=MESH)

        def meet_wait(step):
            if step < meetings:
                pl.semaphore_wait(meet.at[step], 2)

        def meet_last():
            for step in range(2, meetings):
                if step > 2:
                    meet_send(step)
                meet_wait(step)

        def halo(phase, mid_src, mid_dst, edge_src, edge_dst):
            sides = ((1, 0),) if mid_dst is not None else ()
            sides += ((0, 1), (2, -1)) if edge_dst is not None else ()

            def copy_of(d, side, da):
                return pltpu.make_async_remote_copy(
                    src_ref=mid_src if side == 1 else edge_src.at[side // 2],
                    dst_ref=mid_dst(d) if side == 1 else edge_dst.at[d, side // 2],
                    send_sem=halo_send.at[phase, 3 * d + side],
                    recv_sem=halo_recv.at[phase, 3 * d + side],
                    device_id=at(1 - d, da),
                    device_id_type=MESH,
                )

            def of_block(d, act, own=False):
                for side, da in sides:
                    if not (own and side == 1):
                        act(copy_of(d, side, da))

            def to_all(act):
                pl.when(has_down)(lambda: of_block(0, act))
                pl.when(has_up)(lambda: of_block(2, act))
                of_block(1, act, own=True)

            def start():
                to_all(lambda copy: copy.start())

            def wait_recv(d):
                of_block(d, lambda copy: copy.wait_recv(), own=isinstance(d, int))

            def wait_send():
                to_all(lambda copy: copy.wait_send())

            return start, wait_recv, wait_send

        first_halo = halo(0, low_out, lambda d: low_in.at[d], low_edge_out, low_edge_in)
        masked_halo = halo(1, masked.at[1], lambda d: masked.at[d], masked_edge_out, masked_edge)
        removal_halo = halo(3, removal.at[1], lambda d: removal.at[d], removal_edge_out, removal_edge)

        def grad_phase(t):
            mine = pl.ds(t * field, field)
            edges_of = (grad_edge_out, grad_edge_in) if t == 0 else (None, None)
            return halo(4 if t else 2, grad_low.at[mine], lambda d: grad_in.at[d, mine], *edges_of)

        grad_halos = [grad_phase(t) for t in range(tools)]
        near = 2 - 2 * lax.rem(rad, 2)
        far = 2 - near
        has_far = jnp.where(near == 2, rad, rad_count - 1 - rad) > 0

        first_halo[0]()
        meet_send(0)

        influence_copy.wait()
        j_of = lax.broadcasted_iota(jnp.int32, (extent, LANES), 0)
        l_of = lax.broadcasted_iota(jnp.int32, (extent, LANES), 1)

        def spread(rows_of, where_j):
            return jnp.dot(rows_of, (l_of == where_j).astype(BF16), preferred_element_type=F32)

        head_adj[...] = spread(influence_ref[0], j_of) + spread(influence_ref[1], extent + j_of)
        head_fwd[...] = jnp.zeros_like(head_fwd)
        head_two[...] = jnp.zeros_like(head_two)
        for t in range(tools):
            head_fwd[t, 0:extent, :] = spread(influence_ref[t], extent - 1 - j_of)
            head_two[t, 1 : extent + 1, :] = spread(influence_ref[t], 2 * extent - 1 - j_of)
        head_fwd[...] = head_fwd[...] + head_two[...]
        c_of = lax.broadcasted_iota(jnp.int32, (LANES, LANES), 0)
        o_of = lax.broadcasted_iota(jnp.int32, (LANES, LANES), 1)
        low_side = o_of < extent
        off = o_of - c_of
        adj_keep = (low_side & (off >= -extent) & (off < 0)) | (~low_side & (off >= 0) & (off < extent))
        fwd_keep = (low_side & (off > -extent) & (off <= 0)) | (~low_side & (off > 0) & (off <= extent))
        keep[0] = adj_keep.astype(F32)
        keep[1] = fwd_keep.astype(F32)
        blank = jnp.zeros((LANES, LANES), BF16)
        band_adj[0:LANES, :] = blank
        band_adj[LANES : 2 * LANES, :] = blank
        band_adj[(extent + 2) * LANES : (extent + 3) * LANES, :] = blank
        for t in range(tools):
            band_fwd[t, (extent + 1) * LANES : (extent + 2) * LANES, :] = blank

        def toeplitz(head, shift, which):
            square = jnp.broadcast_to(head, (LANES, LANES))
            turned = pltpu.roll(square, shift, axis=1, stride=1, stride_axis=0)
            return (turned * keep[which]).astype(BF16)

        @pl.loop(0, extent, unroll=4)
        def _(i):
            at_i = pl.ds(pl.multiple_of((extent + 1 - i) * LANES, LANES), LANES)
            band_adj[at_i, :] = toeplitz(head_adj[pl.ds(i, 1), :], extent, 0)

        k_of = lax.broadcasted_iota(jnp.int32, (words, LANES), 0)
        b_of = lax.broadcasted_iota(jnp.int32, (words, LANES), 1)
        bits_copy.wait()
        word = bits_ref[...].reshape(tools * rows, words)
        low_byte = (word & 255).astype(F32).astype(BF16)
        high_byte = (word >> 8).astype(F32).astype(BF16)
        for c in range(tiles):
            mine = k_of == c * (LANES // 16) + b_of // 16
            upper = b_of % 16 >= 8
            byte = jnp.dot(low_byte, (mine & ~upper).astype(BF16), preferred_element_type=F32)
            byte += jnp.dot(high_byte, (mine & upper).astype(BF16), preferred_element_type=F32)
            bit_at = lax.broadcasted_iota(jnp.int32, byte.shape, 1) % 8
            allowed[pl.ds(c, tools * rows, stride=tiles), :] = (
                (byte.astype(jnp.int32) >> bit_at) & 1
            ).astype(F32)

        def assemble(target, d, two_rows):
            @pl.loop(0, pairs, unroll=True)
            def _(m):
                both = two_rows(m)
                for a in range(2):
                    row = both[a * tiles : (a + 1) * tiles]
                    before = jnp.broadcast_to(edge[0, pl.ds(2 * m + a, 1), :], (SUB, LANES))
                    after = jnp.broadcast_to(edge[1, pl.ds(2 * m + a, 1), :], (SUB, LANES))
                    prior = jnp.where(sub == 0, before, pltpu.roll(row, 1, axis=0))
                    later = jnp.where(sub == SUB - 1, after, pltpu.roll(row, SUB - 1, axis=0))
                    even = pltpu.roll(jnp.where(lane >= 96, prior, row), 32, axis=1)
                    odd = pltpu.roll(jnp.where(lane < 32, later, row), 96, axis=1)
                    target[
                        pl.ds(pl.multiple_of((pairs * d + m) * 16, 16), 16),
                        a * LANES : (a + 1) * LANES,
                    ] = jnp.concatenate([even, odd], axis=0).astype(BF16)

        def at_pair(m):
            return pl.ds(pl.multiple_of(m * 2 * tiles, 2 * tiles), 2 * tiles)

        def far_block(block, target=None):
            pl.when(has_far)(lambda: block(far))
            if target is not None:

                @pl.when(jnp.logical_not(has_far))
                def _():
                    at_far = pl.ds(pl.multiple_of(far * pairs * 16, pairs * 16), pairs * 16)
                    target[at_far, :] = jnp.zeros((pairs * 16, 2 * LANES), BF16)

        def groups(step, far_ready):
            @pl.loop(0, steps // group)
            def _(i):
                pl.when(i == 1)(far_ready)
                step(near + i * (1 - near))

        def adjoint(out, far_ready):
            acc[...] = jnp.zeros_like(acc)

            def one(kk):
                lhs = jnp.concatenate(
                    [
                        win_adj[pl.ds(pl.multiple_of((group * kk + u) * 16, 16), pairs * 16), :]
                        for u in range(group)
                    ],
                    axis=1,
                )
                first = pl.multiple_of(2 * group * kk * LANES, LANES)
                rhs = jnp.concatenate(
                    [
                        band_adj[pl.ds(first + LANES, 2 * group * LANES), :],
                        band_adj[pl.ds(first, 2 * group * LANES), :],
                    ],
                    axis=1,
                )
                acc[...] += jnp.dot(lhs, rhs, preferred_element_type=F32)

            groups(one, far_ready)

            def finish(m, total):
                for b in range(2):
                    cols = slice(b * LANES, (b + 1) * LANES)
                    even = acc[pl.ds(pl.multiple_of(m * 16, 16), 8), cols]
                    odd = acc[pl.ds(pl.multiple_of(m * 16 + 8, 8), 8), cols]
                    values = (
                        jnp.where(left_half, even, pltpu.roll(odd, 64, axis=1)),
                        jnp.where(left_half, pltpu.roll(even, 64, axis=1), odd),
                    )
                    for t in range(tools):
                        at_r = pl.ds(pl.multiple_of((t * rows + 2 * m + b) * tiles, tiles), tiles)
                        value = allowed[at_r, :] * values[t]
                        out[at_r, :] = value
                        total = total + value * value
                return total

            return lax.fori_loop(0, pairs, finish, jnp.zeros((SUB, LANES), F32), unroll=4)

        def sum_stage(which, source, box, count, peer_of):
            def copy_to(step):
                return pltpu.make_async_remote_copy(
                    src_ref=msg.at[source],
                    dst_ref=box.at[step - 1],
                    send_sem=sum_send.at[which],
                    recv_sem=sum_recv.at[which],
                    device_id=peer_of(step),
                    device_id_type=MESH,
                )

            for step in range(1, count):
                copy_to(step).start()

            all_of = pltpu.make_async_remote_copy(
                src_ref=box,
                dst_ref=box,
                send_sem=sum_send.at[which],
                recv_sem=sum_recv.at[which],
                device_id=peer_of(1),
                device_id_type=MESH,
            )
            return all_of

        def total_of(first, beside_plane, beside_line):
            stage = sum_stage(first, first, box_a.at[first // 2], plane_count, plane_peer)
            beside_plane()
            stage.wait_recv()
            msg[first + 1] = msg[first] + jnp.sum(box_a[first // 2], axis=0)
            other = sum_stage(first + 1, first + 1, box_b.at[first // 2], line_count, line_peer)
            beside_line()
            other.wait_recv()
            everything = msg[first + 1] + jnp.sum(box_b[first // 2], axis=0)
            return jnp.sum(everything, axis=1, keepdims=True), (stage, other)

        def first_block(d):
            first_halo[1](d)
            edge[...] = low_edge_in[d].astype(F32)
            if isinstance(d, int):
                assemble(win_adj, d, lambda m: masked[d, at_pair(m), :])
            else:
                assemble(win_adj, d, lambda m: low_in[d, at_pair(m), :].astype(F32))

        first_block(1)
        first_block(near)

        def first_far():
            far_block(first_block, win_adj)

        gamma_part = adjoint(gradient, first_far)
        grad_low[...] = gradient[...].astype(BF16)
        for side, tile in ((0, tiles - 1), (1, 0)):
            grad_edge_out[side] = gradient[pl.ds(tile, tools * rows, stride=tiles), :].astype(BF16)
        for grad_halo in grad_halos:
            grad_halo[0]()
        meet_wait(0)
        meet_send(1)

        for t in range(tools):

            @pl.loop(0, extent + 1, unroll=5)
            def _(q, t=t):
                at_q = pl.ds(pl.multiple_of(q * LANES, LANES), LANES)
                band_fwd[t, at_q, :] = toeplitz(head_fwd[t, pl.ds(q, 1), :], extent + 1, 1)

        acc_fwd[...] = jnp.zeros_like(acc_fwd)
        for t in range(tools):

            def grad_block(d, t=t):
                grad_halos[t][1](d)
                edge[...] = grad_edge_in[d, :, t * rows : (t + 1) * rows, :].astype(F32)

                def mine(m):
                    return pl.ds(pl.multiple_of(t * field + m * 16, 16), 16)

                if isinstance(d, int):
                    assemble(win_fwd.at[t], d, lambda m: gradient[mine(m), :])
                else:
                    assemble(win_fwd.at[t], d, lambda m: grad_in[d, mine(m), :].astype(F32))

            def one(kk, t=t):
                lhs = jnp.concatenate(
                    [
                        win_fwd[t, pl.ds(pl.multiple_of((group * kk + u) * 16, 16), pairs * 16), :]
                        for u in range(group)
                    ],
                    axis=1,
                )
                first = pl.multiple_of(2 * group * kk * LANES, LANES)
                rhs = band_fwd[t, pl.ds(first, 2 * group * LANES), :]
                acc_fwd[...] += jnp.dot(lhs, rhs, preferred_element_type=F32)

            grad_block(1)
            grad_block(near)
            groups(one, lambda t=t, block=grad_block: far_block(block, win_fwd.at[t]))
            if t == 0:
                masked_halo[0]()

        @pl.loop(0, pairs, unroll=4)
        def _(m):
            even = acc_fwd[pl.ds(pl.multiple_of(m * 16, 16), 8), :]
            odd = acc_fwd[pl.ds(pl.multiple_of(m * 16 + 8, 8), 8), :]
            top = jnp.where(left_half, even, pltpu.roll(odd, 64, axis=1))
            low = jnp.where(left_half, pltpu.roll(even, 64, axis=1), odd)
            at_m = at_pair(m)
            part[at_m, :] = inside[at_m, :] * jnp.concatenate([top, low], axis=0)

        tool_copies = []
        for step in range(1, tool_count):
            tool_copies.append(
                pltpu.make_async_remote_copy(
                    src_ref=part,
                    dst_ref=part_in.at[step - 1],
                    send_sem=tool_sem.at[0, step - 1],
                    recv_sem=tool_sem.at[1, step - 1],
                    device_id={"az": az, "rad": rad, "tool": lax.rem(tool + step, tool_count)},
                    device_id_type=MESH,
                )
            )
        for copy in tool_copies:
            copy.start()
        meet_wait(1)
        meet_send(2)
        for copy in tool_copies:
            copy.wait_recv()

        def join(m, total):
            at_m = at_pair(m)
            value = part[at_m, :]
            for step in range(1, tool_count):
                value = value + part_in[step - 1, at_m, :]
            removal[1, at_m, :] = value
            return total + value[:SUB] * value[:SUB] + value[SUB:] * value[SUB:]

        curvature_part = lax.fori_loop(0, pairs, join, jnp.zeros((SUB, LANES), F32), unroll=4)
        msg[0] = jnp.concatenate(
            [
                jnp.sum(gamma_part, axis=0, keepdims=True),
                jnp.sum(curvature_part, axis=0, keepdims=True),
            ],
            axis=0,
        )

        def edges():
            for side, tile in ((0, tiles - 1), (1, 0)):
                removal_edge_out[side] = removal[1, pl.ds(tile, rows, stride=tiles), :]
            dwell_copy.wait()
            meet_last()

        sums, stages = total_of(0, edges, removal_halo[0])
        gamma = sums[0:1]
        curvature = sums[1:2] * (1.0 / tool_count)
        step_size = gamma / (curvature + EPSILON)

        def second_block(d):
            masked_halo[1](d)
            removal_halo[1](d)
            edge[...] = masked_edge[d] - step_size * removal_edge[d]
            assemble(
                win_adj, d, lambda m: masked[d, at_pair(m), :] - step_size * removal[d, at_pair(m), :]
            )

        second_block(1)
        second_block(near)
        new_part = adjoint(gradient_new, lambda: far_block(second_block))
        new_row = jnp.sum(new_part, axis=0, keepdims=True)
        msg[2] = jnp.concatenate([new_row, new_row], axis=0)

        def dwell_output():
            for t in range(tools):
                for c in range(tiles):
                    cols = slice(c * LANES, (c + 1) * LANES)
                    step_of = gradient[pl.ds(t * field + c, rows, stride=tiles), :]
                    grad_natural[t, :, cols] = step_of
                    dwell_out[t, :, cols] = dwell_v[t, :, cols] + step_size * step_of

        def residual_output():
            for t in range(tools):
                for c in range(tiles):
                    from_c = pl.ds(t * field + c, rows, stride=tiles)
                    direction_out[t, :, c * LANES : (c + 1) * LANES] = gradient_new[from_c, :]
            for c in range(share_tiles):
                from_c = pl.ds(tool * share_tiles + c, rows, stride=tiles)
                residual_out[:, c * LANES : (c + 1) * LANES] = (
                    whole[from_c, :] - step_size * removal[1, from_c, :]
                )

        new_sums, new_stages = total_of(2, dwell_output, residual_output)
        ratio = new_sums[0:1] / (gamma + EPSILON)
        for t in range(tools):
            direction_out[t] = direction_out[t] + ratio * grad_natural[t]

        for phase in (first_halo, masked_halo, *grad_halos, removal_halo):
            phase[2]()
        for copy in tool_copies:
            copy.wait_send()
        for stage in stages + new_stages:
            stage.wait_send()

    hbm_spec = pl.BlockSpec(memory_space=pltpu.HBM)
    scratch = [
        ((rows, width), F32),
        (dwell_shape, F32),
        ((field, LANES), F32),
        ((3, field, LANES), F32),
        ((3, 2, rows, LANES), F32),
        ((2, rows, LANES), F32),
        ((field, LANES), BF16),
        ((2, rows, LANES), BF16),
        ((3, field, LANES), BF16),
        ((3, 2, rows, LANES), BF16),
        ((field, LANES), F32),
        ((tools * field, LANES), F32),
        ((extent, LANES), F32),
        ((tools, extent + 8, LANES), F32),
        ((tools, extent + 8, LANES), F32),
        ((2, LANES, LANES), F32),
        (((extent + 3) * LANES, LANES), BF16),
        ((tools, (extent + 2) * LANES, LANES), BF16),
        ((3 * pairs * 16, 2 * LANES), BF16),
        ((tools, 3 * pairs * 16, 2 * LANES), BF16),
        ((pairs * 16, 2 * LANES), F32),
        ((pairs * 16, LANES), F32),
        ((tools * field, LANES), F32),
        ((tools * field, LANES), BF16),
        ((2, tools * rows, LANES), BF16),
        ((3, tools * field, LANES), BF16),
        ((3, 2, tools * rows, LANES), BF16),
        ((field, LANES), F32),
        ((tool_count - 1, field, LANES), F32),
        ((3, field, LANES), F32),
        ((2, rows, LANES), F32),
        ((3, 2, rows, LANES), F32),
        ((2, rows, LANES), F32),
        ((tools * field, LANES), F32),
        (dwell_shape, F32),
        ((4, 2, LANES), F32),
        ((2, plane_count - 1, 2, LANES), F32),
        ((2, line_count - 1, 2, LANES), F32),
    ]
    return pl.pallas_call(
        body,
        out_shape=(
            pltpu.VMEM(dwell_shape, F32),
            pltpu.VMEM((rows, share), F32),
            pltpu.VMEM(dwell_shape, F32),
        ),
        in_specs=[hbm_spec] * 6,
        out_specs=(pl.BlockSpec(memory_space=pltpu.VMEM),) * 3,
        scratch_shapes=[
            pltpu.VMEM(influence_shape, BF16),
            pltpu.SMEM((rows,), jnp.int32),
            pltpu.SMEM((rows,), jnp.int32),
            pltpu.VMEM((tools, rows, words), jnp.int32),
        ]
        + [pltpu.VMEM(shape, dtype) for shape, dtype in scratch]
        + [
            pltpu.SemaphoreType.DMA((9,)),
            pltpu.SemaphoreType.DMA((5, 9)),
            pltpu.SemaphoreType.DMA((5, 9)),
            pltpu.SemaphoreType.DMA((2, max(tool_count - 1, 1))),
            pltpu.SemaphoreType.REGULAR((max(meetings_of(line_count), 1),)),
            pltpu.SemaphoreType.DMA((4,)),
            pltpu.SemaphoreType.DMA((4,)),
        ],
        compiler_params=pltpu.CompilerParams(
            collective_id=0, has_side_effects=True, vmem_limit_bytes=24 * 1024 * 1024
        ),
        name="cgls",
    )


def hand_on(results):
    count = len(results)

    def body(*refs):
        sem = refs[-1]
        copies = [
            pltpu.make_async_copy(refs[i], refs[count + i], sem.at[i]) for i in range(count)
        ]
        for copy in copies:
            copy.start()
        for copy in copies:
            copy.wait()

    return pl.pallas_call(
        body,
        out_shape=tuple(jax.ShapeDtypeStruct(x.shape, x.dtype) for x in results),
        in_specs=[pl.BlockSpec(memory_space=pl.ANY)] * count,
        out_specs=(pl.BlockSpec(memory_space=pltpu.HBM),) * count,
        scratch_shapes=[pltpu.SemaphoreType.DMA((count,))],
        name="hand_on",
    )(*(pltpu.with_memory_space_constraint(x, pltpu.VMEM) for x in results))


def solution(mesh):
    def per_device(dwell, residual, influence, cycle_start, cycle_end, allowed_bits):
        call = build(
            dwell.shape,
            influence.shape,
            allowed_bits.shape[-1],
            mesh.shape["az"],
            mesh.shape["rad"],
            mesh.shape["tool"],
        )
        given = (dwell, residual, influence, cycle_start, cycle_end, allowed_bits)
        return hand_on(call(*(pltpu.with_memory_space_constraint(x, pltpu.HBM) for x in given)))

    in_specs = (
        P("tool", "rad", "az"),
        P("rad", "az"),
        P("tool", None, None),
        P("rad"),
        P("rad"),
        P("tool", "rad", "az"),
    )
    out_specs = (P("tool", "rad", "az"), P("rad", ("az", "tool")), P("tool", "rad", "az"))
    return jax.shard_map(
        per_device, mesh=mesh, in_specs=in_specs, out_specs=out_specs, check_vma=False
    )
```

```python
import jax
import jax.numpy as jnp
from jax import lax
from jax.experimental import pallas as pl
from jax.experimental.pallas import tpu as pltpu
from jax.sharding import PartitionSpec as P

EPSILON = 1e-06
MESH = pl.DeviceIdType.MESH
F32 = jnp.float32
BF16 = jnp.bfloat16
LANES = 128
SUB = 8


def meetings_of(line_count):
    return max(line_count // 2, 1).bit_length() - 1


def build(dwell_shape, influence_shape, words, az_count, rad_count, tool_count):
    tools, rows, width = dwell_shape
    extent = influence_shape[-1]
    tiles = width // LANES
    assert tiles == SUB and extent == 64 and rows == 32
    pairs = rows // 2
    field = rows * tiles
    steps = extent // 2 + 1
    group = 11
    quads, steps_fwd, group_fwd = rows // 4, extent // 2 + 2, 17
    assert steps % group == 0 and steps_fwd % group_fwd == 0
    plane_count = 2 * rad_count * tool_count
    line_count = az_count // 2
    for count in (az_count, rad_count, tool_count):
        assert count & (count - 1) == 0
    share = width // tool_count
    share_tiles = share // LANES

    def body(
        dwell_hbm,
        residual_hbm,
        influence_hbm,
        start_hbm,
        end_hbm,
        bits_hbm,
        dwell_out,
        residual_out,
        direction_out,
        influence_ref,
        start_ref,
        end_ref,
        bits_ref,
        natural,
        dwell_v,
        whole,
        masked,
        masked_edge,
        masked_edge_out,
        low_out,
        low_edge_out,
        low_in,
        low_edge_in,
        inside,
        allowed,
        head_adj,
        head_fwd,
        head_two,
        keep,
        band_adj,
        band_fwd,
        win_adj,
        win_fwd,
        acc,
        acc_fwd,
        gradient,
        grad_low,
        grad_edge_out,
        grad_in,
        grad_edge_in,
        part,
        part_in,
        removal,
        removal_edge_out,
        removal_edge,
        edge,
        gradient_new,
        grad_natural,
        msg,
        box_a,
        box_b,
        local_sem,
        halo_send,
        halo_recv,
        tool_sem,
        meet,
        sum_send,
        sum_recv,
    ):
        az, rad, tool = lax.axis_index("az"), lax.axis_index("rad"), lax.axis_index("tool")
        lane = lax.broadcasted_iota(jnp.int32, (SUB, LANES), 1)
        sub = lax.broadcasted_iota(jnp.int32, (SUB, LANES), 0)
        left_half = lane < LANES // 2

        residual_copy = pltpu.make_async_copy(residual_hbm, natural, local_sem.at[0])
        start_copy = pltpu.make_async_copy(start_hbm, start_ref, local_sem.at[5])
        end_copy = pltpu.make_async_copy(end_hbm, end_ref, local_sem.at[6])
        influence_copy = pltpu.make_async_copy(influence_hbm, influence_ref, local_sem.at[7])
        bits_copy = pltpu.make_async_copy(bits_hbm, bits_ref, local_sem.at[8])
        dwell_copy = pltpu.make_async_copy(dwell_hbm, dwell_v, local_sem.at[1])
        for copy in (residual_copy, start_copy, end_copy, influence_copy, bits_copy, dwell_copy):
            copy.start()

        def at(dr, da):
            return {
                "az": lax.rem(az + da + az_count, az_count),
                "rad": rad + dr,
                "tool": tool,
            }

        def plane_peer(step):
            return {
                "az": az ^ (step % 2),
                "rad": rad ^ (step // (2 * tool_count)),
                "tool": tool ^ (step // 2 % tool_count),
            }

        def line_peer(step):
            return {"az": az ^ (2 * step), "rad": rad, "tool": tool}

        has_up, has_down = rad > 0, rad < rad_count - 1

        barrier = pltpu.get_barrier_semaphore()

        def greet(peer):
            pl.semaphore_signal(barrier, inc=1, device_id=peer, device_id_type=MESH)

        outer = 1 - 2 * (1 - lax.rem(az, 2))
        greet(at(0, outer))
        greet(at(0, 2))
        greet(at(0, -2))

        @pl.when(has_up)
        def _():
            greet(at(-1, outer))

        @pl.when(has_down)
        def _():
            greet(at(1, outer))

        for step in range(1, plane_count):
            greet(plane_peer(step))

        residual_copy.wait()
        for c in range(tiles):
            whole[pl.ds(c, rows, stride=tiles), :] = natural[:, c * LANES : (c + 1) * LANES]
        start_copy.wait()
        end_copy.wait()
        column = az * width + sub * LANES + lane

        @pl.loop(0, rows, unroll=4)
        def _(r):
            at_r = pl.ds(pl.multiple_of(r * tiles, tiles), tiles)
            valid = ((column >= start_ref[r]) & (column < end_ref[r])).astype(F32)
            inside[at_r, :] = valid
            masked[1, at_r, :] = valid * whole[at_r, :]

        low_out[...] = masked[1].astype(BF16)
        for side, tile in ((0, tiles - 1), (1, 0)):
            tile_of = masked[1, pl.ds(tile, rows, stride=tiles), :]
            masked_edge_out[side] = tile_of
            low_edge_out[side] = tile_of.astype(BF16)

        extra = 1 + has_up.astype(jnp.int32) + has_down.astype(jnp.int32)
        pl.semaphore_wait(barrier, plane_count + 1 + extra)

        meetings = meetings_of(line_count)

        def meet_send(step):
            if step < meetings:
                for da in (2 << step, -(2 << step)):
                    pl.semaphore_signal(meet.at[step], inc=1, device_id=at(0, da), device_id_type=MESH)

        def meet_wait(step):
            if step < meetings:
                pl.semaphore_wait(meet.at[step], 2)

        def meet_last():
            for step in range(2, meetings):
                if step > 2:
                    meet_send(step)
                meet_wait(step)

        def halo(phase, mid_src, mid_dst, edge_src, edge_dst):
            sides = ((1, 0),) if mid_dst is not None else ()
            sides += ((0, 1), (2, -1)) if edge_dst is not None else ()

            def copy_of(d, side, da):
                return pltpu.make_async_remote_copy(
                    src_ref=mid_src if side == 1 else edge_src.at[side // 2],
                    dst_ref=mid_dst(d) if side == 1 else edge_dst.at[d, side // 2],
                    send_sem=halo_send.at[phase, 3 * d + side],
                    recv_sem=halo_recv.at[phase, 3 * d + side],
                    device_id=at(1 - d, da),
                    device_id_type=MESH,
                )

            def of_block(d, act, own=False):
                for side, da in sides:
                    if not (own and side == 1):
                        act(copy_of(d, side, da))

            def to_all(act):
                pl.when(has_down)(lambda: of_block(0, act))
                pl.when(has_up)(lambda: of_block(2, act))
                of_block(1, act, own=True)

            def start():
                to_all(lambda copy: copy.start())

            def wait_recv(d):
                of_block(d, lambda copy: copy.wait_recv(), own=isinstance(d, int))

            def wait_send():
                to_all(lambda copy: copy.wait_send())

            return start, wait_recv, wait_send

        first_halo = halo(0, low_out, lambda d: low_in.at[d], low_edge_out, low_edge_in)
        masked_halo = halo(1, masked.at[1], lambda d: masked.at[d], masked_edge_out, masked_edge)
        removal_halo = halo(3, removal.at[1], lambda d: removal.at[d], removal_edge_out, removal_edge)

        def grad_phase(t):
            mine = pl.ds(t * field, field)
            edges_of = (grad_edge_out, grad_edge_in) if t == 0 else (None, None)
            return halo(4 if t else 2, grad_low.at[mine], lambda d: grad_in.at[d, mine], *edges_of)

        grad_halos = [grad_phase(t) for t in range(tools)]
        near = 2 - 2 * lax.rem(rad, 2)
        far = 2 - near
        has_far = jnp.where(near == 2, rad, rad_count - 1 - rad) > 0

        first_halo[0]()
        meet_send(0)

        influence_copy.wait()
        j_of = lax.broadcasted_iota(jnp.int32, (extent, LANES), 0)
        l_of = lax.broadcasted_iota(jnp.int32, (extent, LANES), 1)

        def spread(rows_of, where_j):
            return jnp.dot(rows_of, (l_of == where_j).astype(BF16), preferred_element_type=F32)

        head_adj[...] = spread(influence_ref[0], j_of) + spread(influence_ref[1], extent + j_of)
        head_fwd[...] = jnp.zeros_like(head_fwd)
        head_two[...] = jnp.zeros_like(head_two)
        for t in range(tools):
            head_fwd[t, 0:extent, :] = spread(influence_ref[t], extent - 1 - j_of)
            head_two[t, 1 : extent + 1, :] = spread(influence_ref[t], 2 * extent - 1 - j_of)
        head_fwd[...] = head_fwd[...] + head_two[...]
        c_of = lax.broadcasted_iota(jnp.int32, (LANES, LANES), 0)
        o_of = lax.broadcasted_iota(jnp.int32, (LANES, LANES), 1)
        low_side = o_of < extent
        off = o_of - c_of
        adj_keep = (low_side & (off >= -extent) & (off < 0)) | (~low_side & (off >= 0) & (off < extent))
        fwd_keep = (low_side & (off > -extent) & (off <= 0)) | (~low_side & (off > 0) & (off <= extent))
        keep[0] = adj_keep.astype(F32)
        keep[1] = fwd_keep.astype(F32)
        blank = jnp.zeros((LANES, LANES), BF16)
        band_adj[0:LANES, :] = blank
        band_adj[LANES : 2 * LANES, :] = blank
        band_adj[(extent + 2) * LANES : (extent + 3) * LANES, :] = blank
        for t in range(tools):
            band_fwd[t, 0 : 2 * LANES, :] = jnp.zeros((2 * LANES, LANES), BF16)
            band_fwd[t, (extent + 3) * LANES :, :] = jnp.zeros((3 * LANES, LANES), BF16)

        def toeplitz(head, shift, which):
            square = jnp.broadcast_to(head, (LANES, LANES))
            turned = pltpu.roll(square, shift, axis=1, stride=1, stride_axis=0)
            return (turned * keep[which]).astype(BF16)

        @pl.loop(0, extent, unroll=4)
        def _(i):
            at_i = pl.ds(pl.multiple_of((extent + 1 - i) * LANES, LANES), LANES)
            band_adj[at_i, :] = toeplitz(head_adj[pl.ds(i, 1), :], extent, 0)

        k_of = lax.broadcasted_iota(jnp.int32, (words, LANES), 0)
        b_of = lax.broadcasted_iota(jnp.int32, (words, LANES), 1)
        bits_copy.wait()
        word = bits_ref[...].reshape(tools * rows, words)
        low_byte = (word & 255).astype(F32).astype(BF16)
        high_byte = (word >> 8).astype(F32).astype(BF16)
        for c in range(tiles):
            mine = k_of == c * (LANES // 16) + b_of // 16
            upper = b_of % 16 >= 8
            byte = jnp.dot(low_byte, (mine & ~upper).astype(BF16), preferred_element_type=F32)
            byte += jnp.dot(high_byte, (mine & upper).astype(BF16), preferred_element_type=F32)
            bit_at = lax.broadcasted_iota(jnp.int32, byte.shape, 1) % 8
            allowed[pl.ds(c, tools * rows, stride=tiles), :] = (
                (byte.astype(jnp.int32) >> bit_at) & 1
            ).astype(F32)

        def assemble(target, d, two_rows):
            @pl.loop(0, pairs, unroll=True)
            def _(m):
                both = two_rows(m)
                for a in range(2):
                    row = both[a * tiles : (a + 1) * tiles]
                    before = jnp.broadcast_to(edge[0, pl.ds(2 * m + a, 1), :], (SUB, LANES))
                    after = jnp.broadcast_to(edge[1, pl.ds(2 * m + a, 1), :], (SUB, LANES))
                    prior = jnp.where(sub == 0, before, pltpu.roll(row, 1, axis=0))
                    later = jnp.where(sub == SUB - 1, after, pltpu.roll(row, SUB - 1, axis=0))
                    even = pltpu.roll(jnp.where(lane >= 96, prior, row), 32, axis=1)
                    odd = pltpu.roll(jnp.where(lane < 32, later, row), 96, axis=1)
                    target[
                        pl.ds(pl.multiple_of((pairs * d + m) * 16, 16), 16),
                        a * LANES : (a + 1) * LANES,
                    ] = jnp.concatenate([even, odd], axis=0).astype(BF16)

        def at_pair(m):
            return pl.ds(pl.multiple_of(m * 2 * tiles, 2 * tiles), 2 * tiles)

        def far_block(block, target=None):
            pl.when(has_far)(lambda: block(far))
            if target is not None:

                @pl.when(jnp.logical_not(has_far))
                def _():
                    at_far = pl.ds(pl.multiple_of(far * pairs * 16, pairs * 16), pairs * 16)
                    target[at_far, :] = jnp.zeros((pairs * 16, 2 * LANES), BF16)

        def groups(count, step, far_ready):
            @pl.loop(0, count)
            def _(i):
                pl.when(i == 1)(far_ready)
                step(near // 2 * (count - 1) + i * (1 - near))

        def adjoint(out, far_ready):
            acc[...] = jnp.zeros_like(acc)

            def one(kk):
                lhs = jnp.concatenate(
                    [
                        win_adj[pl.ds(pl.multiple_of((group * kk + u) * 16, 16), pairs * 16), :]
                        for u in range(group)
                    ],
                    axis=1,
                )
                first = pl.multiple_of(2 * group * kk * LANES, LANES)
                rhs = jnp.concatenate(
                    [
                        band_adj[pl.ds(first + LANES, 2 * group * LANES), :],
                        band_adj[pl.ds(first, 2 * group * LANES), :],
                    ],
                    axis=1,
                )
                acc[...] += jnp.dot(lhs, rhs, preferred_element_type=F32)

            groups(steps // group, one, far_ready)

            def finish(m, total):
                for b in range(2):
                    cols = slice(b * LANES, (b + 1) * LANES)
                    even = acc[pl.ds(pl.multiple_of(m * 16, 16), 8), cols]
                    odd = acc[pl.ds(pl.multiple_of(m * 16 + 8, 8), 8), cols]
                    values = (
                        jnp.where(left_half, even, pltpu.roll(odd, 64, axis=1)),
                        jnp.where(left_half, pltpu.roll(even, 64, axis=1), odd),
                    )
                    for t in range(tools):
                        at_r = pl.ds(pl.multiple_of((t * rows + 2 * m + b) * tiles, tiles), tiles)
                        value = allowed[at_r, :] * values[t]
                        out[at_r, :] = value
                        total = total + value * value
                return total

            return lax.fori_loop(0, pairs, finish, jnp.zeros((SUB, LANES), F32), unroll=4)

        def sum_stage(which, source, box, count, peer_of):
            def copy_to(step):
                return pltpu.make_async_remote_copy(
                    src_ref=msg.at[source],
                    dst_ref=box.at[step - 1],
                    send_sem=sum_send.at[which],
                    recv_sem=sum_recv.at[which],
                    device_id=peer_of(step),
                    device_id_type=MESH,
                )

            for step in range(1, count):
                copy_to(step).start()

            all_of = pltpu.make_async_remote_copy(
                src_ref=box,
                dst_ref=box,
                send_sem=sum_send.at[which],
                recv_sem=sum_recv.at[which],
                device_id=peer_of(1),
                device_id_type=MESH,
            )
            return all_of

        def total_of(first, beside_plane, beside_line):
            stage = sum_stage(first, first, box_a.at[first // 2], plane_count, plane_peer)
            beside_plane()
            stage.wait_recv()
            msg[first + 1] = msg[first] + jnp.sum(box_a[first // 2], axis=0)
            other = sum_stage(first + 1, first + 1, box_b.at[first // 2], line_count, line_peer)
            beside_line()
            other.wait_recv()
            everything = msg[first + 1] + jnp.sum(box_b[first // 2], axis=0)
            return jnp.sum(everything, axis=1, keepdims=True), (stage, other)

        def first_block(d):
            first_halo[1](d)
            edge[...] = low_edge_in[d].astype(F32)
            if isinstance(d, int):
                assemble(win_adj, d, lambda m: masked[d, at_pair(m), :])
            else:
                assemble(win_adj, d, lambda m: low_in[d, at_pair(m), :].astype(F32))

        first_block(1)
        first_block(near)

        def first_far():
            far_block(first_block, win_adj)

        gamma_part = adjoint(gradient, first_far)
        grad_low[...] = gradient[...].astype(BF16)
        for side, tile in ((0, tiles - 1), (1, 0)):
            grad_edge_out[side] = gradient[pl.ds(tile, tools * rows, stride=tiles), :].astype(BF16)
        for grad_halo in grad_halos:
            grad_halo[0]()
        meet_wait(0)
        meet_send(1)

        for t in range(tools):

            @pl.loop(0, extent + 1, unroll=5)
            def _(q, t=t):
                at_q = pl.ds(pl.multiple_of((q + 2) * LANES, LANES), LANES)
                band_fwd[t, at_q, :] = toeplitz(head_fwd[t, pl.ds(q, 1), :], extent + 1, 1)

        acc_fwd[...] = jnp.zeros_like(acc_fwd)
        for t in range(tools):

            def grad_block(d, t=t):
                grad_halos[t][1](d)
                edge[...] = grad_edge_in[d, :, t * rows : (t + 1) * rows, :].astype(F32)

                def mine(m):
                    return pl.ds(pl.multiple_of(t * field + m * 16, 16), 16)

                if isinstance(d, int):
                    assemble(win_fwd.at[t], d, lambda m: gradient[mine(m), :])
                else:
                    assemble(win_fwd.at[t], d, lambda m: grad_in[d, mine(m), :].astype(F32))

            def one(kk, t=t):
                def rows_of(u):
                    return jnp.concatenate(
                        [
                            win_fwd[t, pl.ds(pl.multiple_of((group_fwd * kk + u + 2 * m) * 16, 16), 16), :]
                            for m in range(quads)
                        ],
                        axis=0,
                    )

                lhs = jnp.concatenate([rows_of(u) for u in range(group_fwd)], axis=1)
                first = pl.multiple_of(2 * group_fwd * kk * LANES, LANES)
                span = 2 * group_fwd * LANES
                rhs = jnp.concatenate(
                    [band_fwd[t, pl.ds(first + 2 * LANES, span), :], band_fwd[t, pl.ds(first, span), :]],
                    axis=1,
                )
                acc_fwd[...] += jnp.dot(lhs, rhs, preferred_element_type=F32)

            grad_block(1)
            grad_block(near)
            groups(steps_fwd // group_fwd, one, lambda t=t, block=grad_block: far_block(block, win_fwd.at[t]))
            if t == 0:
                masked_halo[0]()

        @pl.loop(0, quads, unroll=4)
        def _(m):
            for h in range(2):
                cols = slice(h * LANES, (h + 1) * LANES)
                even = acc_fwd[pl.ds(pl.multiple_of(m * 16, 16), 8), cols]
                odd = acc_fwd[pl.ds(pl.multiple_of(m * 16 + 8, 8), 8), cols]
                top = jnp.where(left_half, even, pltpu.roll(odd, 64, axis=1))
                low = jnp.where(left_half, pltpu.roll(even, 64, axis=1), odd)
                at_m = at_pair(2 * m + h)
                part[at_m, :] = inside[at_m, :] * jnp.concatenate([top, low], axis=0)

        tool_copies = []
        for step in range(1, tool_count):
            tool_copies.append(
                pltpu.make_async_remote_copy(
                    src_ref=part,
                    dst_ref=part_in.at[step - 1],
                    send_sem=tool_sem.at[0, step - 1],
                    recv_sem=tool_sem.at[1, step - 1],
                    device_id={"az": az, "rad": rad, "tool": lax.rem(tool + step, tool_count)},
                    device_id_type=MESH,
                )
            )
        for copy in tool_copies:
            copy.start()
        meet_wait(1)
        meet_send(2)
        for copy in tool_copies:
            copy.wait_recv()

        def join(m, total):
            at_m = at_pair(m)
            value = part[at_m, :]
            for step in range(1, tool_count):
                value = value + part_in[step - 1, at_m, :]
            removal[1, at_m, :] = value
            return total + value[:SUB] * value[:SUB] + value[SUB:] * value[SUB:]

        curvature_part = lax.fori_loop(0, pairs, join, jnp.zeros((SUB, LANES), F32), unroll=4)
        msg[0] = jnp.concatenate(
            [
                jnp.sum(gamma_part, axis=0, keepdims=True),
                jnp.sum(curvature_part, axis=0, keepdims=True),
            ],
            axis=0,
        )

        def edges():
            for side, tile in ((0, tiles - 1), (1, 0)):
                removal_edge_out[side] = removal[1, pl.ds(tile, rows, stride=tiles), :]
            dwell_copy.wait()
            meet_last()

        sums, stages = total_of(0, edges, removal_halo[0])
        gamma = sums[0:1]
        curvature = sums[1:2] * (1.0 / tool_count)
        step_size = gamma / (curvature + EPSILON)

        def second_block(d):
            masked_halo[1](d)
            removal_halo[1](d)
            edge[...] = masked_edge[d] - step_size * removal_edge[d]
            assemble(
                win_adj, d, lambda m: masked[d, at_pair(m), :] - step_size * removal[d, at_pair(m), :]
            )

        second_block(1)
        second_block(near)
        new_part = adjoint(gradient_new, lambda: far_block(second_block))
        new_row = jnp.sum(new_part, axis=0, keepdims=True)
        msg[2] = jnp.concatenate([new_row, new_row], axis=0)

        def dwell_output():
            for t in range(tools):
                for c in range(tiles):
                    cols = slice(c * LANES, (c + 1) * LANES)
                    step_of = gradient[pl.ds(t * field + c, rows, stride=tiles), :]
                    grad_natural[t, :, cols] = step_of
                    dwell_out[t, :, cols] = dwell_v[t, :, cols] + step_size * step_of

        def residual_output():
            for t in range(tools):
                for c in range(tiles):
                    from_c = pl.ds(t * field + c, rows, stride=tiles)
                    direction_out[t, :, c * LANES : (c + 1) * LANES] = gradient_new[from_c, :]
            for c in range(share_tiles):
                from_c = pl.ds(tool * share_tiles + c, rows, stride=tiles)
                residual_out[:, c * LANES : (c + 1) * LANES] = (
                    whole[from_c, :] - step_size * removal[1, from_c, :]
                )

        new_sums, new_stages = total_of(2, dwell_output, residual_output)
        ratio = new_sums[0:1] / (gamma + EPSILON)
        for t in range(tools):
            direction_out[t] = direction_out[t] + ratio * grad_natural[t]

        for phase in (first_halo, masked_halo, *grad_halos, removal_halo):
            phase[2]()
        for copy in tool_copies:
            copy.wait_send()
        for stage in stages + new_stages:
            stage.wait_send()

    hbm_spec = pl.BlockSpec(memory_space=pltpu.HBM)
    scratch = [
        ((rows, width), F32),
        (dwell_shape, F32),
        ((field, LANES), F32),
        ((3, field, LANES), F32),
        ((3, 2, rows, LANES), F32),
        ((2, rows, LANES), F32),
        ((field, LANES), BF16),
        ((2, rows, LANES), BF16),
        ((3, field, LANES), BF16),
        ((3, 2, rows, LANES), BF16),
        ((field, LANES), F32),
        ((tools * field, LANES), F32),
        ((extent, LANES), F32),
        ((tools, extent + 8, LANES), F32),
        ((tools, extent + 8, LANES), F32),
        ((2, LANES, LANES), F32),
        (((extent + 3) * LANES, LANES), BF16),
        ((tools, (extent + 6) * LANES, LANES), BF16),
        ((3 * pairs * 16, 2 * LANES), BF16),
        ((tools, 3 * pairs * 16, 2 * LANES), BF16),
        ((pairs * 16, 2 * LANES), F32),
        ((quads * 16, 2 * LANES), F32),
        ((tools * field, LANES), F32),
        ((tools * field, LANES), BF16),
        ((2, tools * rows, LANES), BF16),
        ((3, tools * field, LANES), BF16),
        ((3, 2, tools * rows, LANES), BF16),
        ((field, LANES), F32),
        ((tool_count - 1, field, LANES), F32),
        ((3, field, LANES), F32),
        ((2, rows, LANES), F32),
        ((3, 2, rows, LANES), F32),
        ((2, rows, LANES), F32),
        ((tools * field, LANES), F32),
        (dwell_shape, F32),
        ((4, 2, LANES), F32),
        ((2, plane_count - 1, 2, LANES), F32),
        ((2, line_count - 1, 2, LANES), F32),
    ]
    return pl.pallas_call(
        body,
        out_shape=(
            pltpu.VMEM(dwell_shape, F32),
            pltpu.VMEM((rows, share), F32),
            pltpu.VMEM(dwell_shape, F32),
        ),
        in_specs=[hbm_spec] * 6,
        out_specs=(pl.BlockSpec(memory_space=pltpu.VMEM),) * 3,
        scratch_shapes=[
            pltpu.VMEM(influence_shape, BF16),
            pltpu.SMEM((rows,), jnp.int32),
            pltpu.SMEM((rows,), jnp.int32),
            pltpu.VMEM((tools, rows, words), jnp.int32),
        ]
        + [pltpu.VMEM(shape, dtype) for shape, dtype in scratch]
        + [
            pltpu.SemaphoreType.DMA((9,)),
            pltpu.SemaphoreType.DMA((5, 9)),
            pltpu.SemaphoreType.DMA((5, 9)),
            pltpu.SemaphoreType.DMA((2, max(tool_count - 1, 1))),
            pltpu.SemaphoreType.REGULAR((max(meetings_of(line_count), 1),)),
            pltpu.SemaphoreType.DMA((4,)),
            pltpu.SemaphoreType.DMA((4,)),
        ],
        compiler_params=pltpu.CompilerParams(
            collective_id=0, has_side_effects=True, vmem_limit_bytes=24 * 1024 * 1024
        ),
        name="cgls",
    )


def hand_on(results):
    count = len(results)

    def body(*refs):
        sem = refs[-1]
        copies = [
            pltpu.make_async_copy(refs[i], refs[count + i], sem.at[i]) for i in range(count)
        ]
        for copy in copies:
            copy.start()
        for copy in copies:
            copy.wait()

    return pl.pallas_call(
        body,
        out_shape=tuple(jax.ShapeDtypeStruct(x.shape, x.dtype) for x in results),
        in_specs=[pl.BlockSpec(memory_space=pl.ANY)] * count,
        out_specs=(pl.BlockSpec(memory_space=pltpu.HBM),) * count,
        scratch_shapes=[pltpu.SemaphoreType.DMA((count,))],
        name="hand_on",
    )(*(pltpu.with_memory_space_constraint(x, pltpu.VMEM) for x in results))


def solution(mesh):
    def per_device(dwell, residual, influence, cycle_start, cycle_end, allowed_bits):
        call = build(
            dwell.shape,
            influence.shape,
            allowed_bits.shape[-1],
            mesh.shape["az"],
            mesh.shape["rad"],
            mesh.shape["tool"],
        )
        given = (dwell, residual, influence, cycle_start, cycle_end, allowed_bits)
        return hand_on(call(*(pltpu.with_memory_space_constraint(x, pltpu.HBM) for x in given)))

    in_specs = (
        P("tool", "rad", "az"),
        P("rad", "az"),
        P("tool", None, None),
        P("rad"),
        P("rad"),
        P("tool", "rad", "az"),
    )
    out_specs = (P("tool", "rad", "az"), P("rad", ("az", "tool")), P("tool", "rad", "az"))
    return jax.shard_map(
        per_device, mesh=mesh, in_specs=in_specs, out_specs=out_specs, check_vma=False
    )
```

```python
import jax
import jax.numpy as jnp
from jax import lax
from jax.experimental import pallas as pl
from jax.experimental.pallas import tpu as pltpu
from jax.sharding import PartitionSpec as P

EPSILON = 1e-06
MESH = pl.DeviceIdType.MESH
F32 = jnp.float32
BF16 = jnp.bfloat16
LANES = 128
SUB = 8


def meetings_of(line_count):
    return max(line_count // 2, 1).bit_length() - 1


def build(dwell_shape, influence_shape, words, az_count, rad_count, tool_count):
    tools, rows, width = dwell_shape
    extent = influence_shape[-1]
    tiles = width // LANES
    assert tiles == SUB and extent == 64 and rows == 32
    pairs = rows // 2
    field = rows * tiles
    steps = extent // 2 + 1
    group = 11
    quads, steps_fwd, group_fwd = rows // 4, extent // 2 + 2, 17
    assert steps % group == 0 and steps_fwd % group_fwd == 0
    plane_count = 2 * rad_count * tool_count
    line_count = az_count // 2
    for count in (az_count, rad_count, tool_count):
        assert count & (count - 1) == 0
    share = width // tool_count
    share_tiles = share // LANES

    def body(
        dwell_hbm,
        residual_hbm,
        influence_hbm,
        start_hbm,
        end_hbm,
        bits_hbm,
        dwell_out,
        residual_out,
        direction_out,
        influence_ref,
        start_ref,
        end_ref,
        bits_ref,
        natural,
        dwell_v,
        whole,
        masked,
        masked_edge,
        masked_edge_out,
        low_out,
        low_edge_out,
        low_in,
        low_edge_in,
        inside,
        allowed,
        head_adj,
        head_fwd,
        head_two,
        keep,
        band_adj,
        band_fwd,
        win_adj,
        win_fwd,
        acc,
        acc_fwd,
        gradient,
        grad_low,
        grad_edge_out,
        grad_in,
        grad_edge_in,
        part,
        part_in,
        removal,
        removal_edge_out,
        removal_edge,
        edge,
        gradient_new,
        grad_natural,
        msg,
        box_a,
        box_b,
        local_sem,
        halo_send,
        halo_recv,
        tool_sem,
        meet,
        plane_meet,
        sum_send,
        sum_recv,
    ):
        az, rad, tool = lax.axis_index("az"), lax.axis_index("rad"), lax.axis_index("tool")
        lane = lax.broadcasted_iota(jnp.int32, (SUB, LANES), 1)
        sub = lax.broadcasted_iota(jnp.int32, (SUB, LANES), 0)
        left_half = lane < LANES // 2

        residual_copy = pltpu.make_async_copy(residual_hbm, natural, local_sem.at[0])
        start_copy = pltpu.make_async_copy(start_hbm, start_ref, local_sem.at[5])
        end_copy = pltpu.make_async_copy(end_hbm, end_ref, local_sem.at[6])
        influence_copy = pltpu.make_async_copy(influence_hbm, influence_ref, local_sem.at[7])
        bits_copy = pltpu.make_async_copy(bits_hbm, bits_ref, local_sem.at[8])
        dwell_copy = pltpu.make_async_copy(dwell_hbm, dwell_v, local_sem.at[1])
        for copy in (residual_copy, start_copy, end_copy, influence_copy, bits_copy, dwell_copy):
            copy.start()

        def at(dr, da):
            return {
                "az": lax.rem(az + da + az_count, az_count),
                "rad": rad + dr,
                "tool": tool,
            }

        def plane_peer(step):
            return {
                "az": az ^ (step % 2),
                "rad": rad ^ (step // (2 * tool_count)),
                "tool": tool ^ (step // 2 % tool_count),
            }

        def line_peer(step):
            return {"az": az ^ (2 * step), "rad": rad, "tool": tool}

        has_up, has_down = rad > 0, rad < rad_count - 1

        barrier = pltpu.get_barrier_semaphore()

        def greet(peer):
            pl.semaphore_signal(barrier, inc=1, device_id=peer, device_id_type=MESH)

        for da in (1, -1, 2, -2):
            greet(at(0, da))
        for step in range(1, tool_count):
            greet({"az": az, "rad": rad, "tool": tool ^ step})
        for there, dr in ((has_up, -1), (has_down, 1)):

            @pl.when(there)
            def _(dr=dr):
                for da in (0, 1, -1):
                    greet(at(dr, da))

        residual_copy.wait()
        for c in range(tiles):
            whole[pl.ds(c, rows, stride=tiles), :] = natural[:, c * LANES : (c + 1) * LANES]
        start_copy.wait()
        end_copy.wait()
        column = az * width + sub * LANES + lane

        @pl.loop(0, rows, unroll=4)
        def _(r):
            at_r = pl.ds(pl.multiple_of(r * tiles, tiles), tiles)
            valid = ((column >= start_ref[r]) & (column < end_ref[r])).astype(F32)
            inside[at_r, :] = valid
            masked[1, at_r, :] = valid * whole[at_r, :]

        low_out[...] = masked[1].astype(BF16)
        for side, tile in ((0, tiles - 1), (1, 0)):
            tile_of = masked[1, pl.ds(tile, rows, stride=tiles), :]
            masked_edge_out[side] = tile_of
            low_edge_out[side] = tile_of.astype(BF16)

        beside = has_up.astype(jnp.int32) + has_down.astype(jnp.int32)
        pl.semaphore_wait(barrier, 3 + tool_count + 3 * beside)

        rad_meetings = (rad_count - 1).bit_length()

        def tell(which, peer):
            pl.semaphore_signal(plane_meet.at[which], inc=1, device_id=peer, device_id_type=MESH)

        def rad_send(step):
            if step < rad_meetings:
                reach = 1 << step
                pl.when(rad >= reach)(lambda: tell(step, at(-reach, 0)))
                pl.when(rad + reach < rad_count)(lambda: tell(step, at(reach, 0)))

        def rad_wait(step):
            if step < rad_meetings:
                reach = 1 << step
                known = (rad >= reach).astype(jnp.int32) + (rad + reach < rad_count).astype(jnp.int32)
                pl.semaphore_wait(plane_meet.at[step], known)

        def cross_send(step):
            if step == 0:
                for other in range(1, tool_count):
                    tell(rad_meetings, {"az": az, "rad": rad, "tool": tool ^ other})
            tell(rad_meetings + step, {"az": az ^ 1, "rad": rad, "tool": tool})

        def cross_wait(step):
            pl.semaphore_wait(plane_meet.at[rad_meetings + step], 1 if step else tool_count)

        meetings = meetings_of(line_count)

        def meet_send(step):
            if step < meetings:
                for da in (2 << step, -(2 << step)):
                    pl.semaphore_signal(meet.at[step], inc=1, device_id=at(0, da), device_id_type=MESH)

        def meet_wait(step):
            if step < meetings:
                pl.semaphore_wait(meet.at[step], 2)

        def meet_last():
            for step in range(2, meetings):
                if step > 2:
                    meet_send(step)
                meet_wait(step)

        def halo(phase, mid_src, mid_dst, edge_src, edge_dst):
            sides = ((1, 0),) if mid_dst is not None else ()
            sides += ((0, 1), (2, -1)) if edge_dst is not None else ()

            def copy_of(d, side, da):
                return pltpu.make_async_remote_copy(
                    src_ref=mid_src if side == 1 else edge_src.at[side // 2],
                    dst_ref=mid_dst(d) if side == 1 else edge_dst.at[d, side // 2],
                    send_sem=halo_send.at[phase, 3 * d + side],
                    recv_sem=halo_recv.at[phase, 3 * d + side],
                    device_id=at(1 - d, da),
                    device_id_type=MESH,
                )

            def of_block(d, act, own=False):
                for side, da in sides:
                    if not (own and side == 1):
                        act(copy_of(d, side, da))

            def to_all(act):
                pl.when(has_down)(lambda: of_block(0, act))
                pl.when(has_up)(lambda: of_block(2, act))
                of_block(1, act, own=True)

            def start():
                to_all(lambda copy: copy.start())

            def wait_recv(d):
                of_block(d, lambda copy: copy.wait_recv(), own=isinstance(d, int))

            def wait_send():
                to_all(lambda copy: copy.wait_send())

            return start, wait_recv, wait_send

        first_halo = halo(0, low_out, lambda d: low_in.at[d], low_edge_out, low_edge_in)
        masked_halo = halo(1, masked.at[1], lambda d: masked.at[d], masked_edge_out, masked_edge)
        removal_halo = halo(3, removal.at[1], lambda d: removal.at[d], removal_edge_out, removal_edge)

        def grad_phase(t):
            mine = pl.ds(t * field, field)
            edges_of = (grad_edge_out, grad_edge_in) if t == 0 else (None, None)
            return halo(4 if t else 2, grad_low.at[mine], lambda d: grad_in.at[d, mine], *edges_of)

        grad_halos = [grad_phase(t) for t in range(tools)]
        near = 2 - 2 * lax.rem(rad, 2)
        far = 2 - near
        has_far = jnp.where(near == 2, rad, rad_count - 1 - rad) > 0

        first_halo[0]()
        meet_send(0)
        rad_send(0)

        influence_copy.wait()
        j_of = lax.broadcasted_iota(jnp.int32, (extent, LANES), 0)
        l_of = lax.broadcasted_iota(jnp.int32, (extent, LANES), 1)

        def spread(rows_of, where_j):
            return jnp.dot(rows_of, (l_of == where_j).astype(BF16), preferred_element_type=F32)

        head_adj[...] = spread(influence_ref[0], j_of) + spread(influence_ref[1], extent + j_of)
        head_fwd[...] = jnp.zeros_like(head_fwd)
        head_two[...] = jnp.zeros_like(head_two)
        for t in range(tools):
            head_fwd[t, 0:extent, :] = spread(influence_ref[t], extent - 1 - j_of)
            head_two[t, 1 : extent + 1, :] = spread(influence_ref[t], 2 * extent - 1 - j_of)
        head_fwd[...] = head_fwd[...] + head_two[...]
        c_of = lax.broadcasted_iota(jnp.int32, (LANES, LANES), 0)
        o_of = lax.broadcasted_iota(jnp.int32, (LANES, LANES), 1)
        low_side = o_of < extent
        off = o_of - c_of
        adj_keep = (low_side & (off >= -extent) & (off < 0)) | (~low_side & (off >= 0) & (off < extent))
        fwd_keep = (low_side & (off > -extent) & (off <= 0)) | (~low_side & (off > 0) & (off <= extent))
        keep[0] = adj_keep.astype(F32)
        keep[1] = fwd_keep.astype(F32)
        blank = jnp.zeros((LANES, LANES), BF16)
        band_adj[0:LANES, :] = blank
        band_adj[LANES : 2 * LANES, :] = blank
        band_adj[(extent + 2) * LANES : (extent + 3) * LANES, :] = blank
        for t in range(tools):
            band_fwd[t, 0 : 2 * LANES, :] = jnp.zeros((2 * LANES, LANES), BF16)
            band_fwd[t, (extent + 3) * LANES :, :] = jnp.zeros((3 * LANES, LANES), BF16)

        def toeplitz(head, shift, which):
            square = jnp.broadcast_to(head, (LANES, LANES))
            turned = pltpu.roll(square, shift, axis=1, stride=1, stride_axis=0)
            return (turned * keep[which]).astype(BF16)

        @pl.loop(0, extent, unroll=4)
        def _(i):
            at_i = pl.ds(pl.multiple_of((extent + 1 - i) * LANES, LANES), LANES)
            band_adj[at_i, :] = toeplitz(head_adj[pl.ds(i, 1), :], extent, 0)

        k_of = lax.broadcasted_iota(jnp.int32, (words, LANES), 0)
        b_of = lax.broadcasted_iota(jnp.int32, (words, LANES), 1)
        bits_copy.wait()
        word = bits_ref[...].reshape(tools * rows, words)
        low_byte = (word & 255).astype(F32).astype(BF16)
        high_byte = (word >> 8).astype(F32).astype(BF16)
        for c in range(tiles):
            mine = k_of == c * (LANES // 16) + b_of // 16
            upper = b_of % 16 >= 8
            byte = jnp.dot(low_byte, (mine & ~upper).astype(BF16), preferred_element_type=F32)
            byte += jnp.dot(high_byte, (mine & upper).astype(BF16), preferred_element_type=F32)
            bit_at = lax.broadcasted_iota(jnp.int32, byte.shape, 1) % 8
            allowed[pl.ds(c, tools * rows, stride=tiles), :] = (
                (byte.astype(jnp.int32) >> bit_at) & 1
            ).astype(F32)

        def assemble(target, d, two_rows):
            @pl.loop(0, pairs, unroll=True)
            def _(m):
                both = two_rows(m)
                for a in range(2):
                    row = both[a * tiles : (a + 1) * tiles]
                    before = jnp.broadcast_to(edge[0, pl.ds(2 * m + a, 1), :], (SUB, LANES))
                    after = jnp.broadcast_to(edge[1, pl.ds(2 * m + a, 1), :], (SUB, LANES))
                    prior = jnp.where(sub == 0, before, pltpu.roll(row, 1, axis=0))
                    later = jnp.where(sub == SUB - 1, after, pltpu.roll(row, SUB - 1, axis=0))
                    even = pltpu.roll(jnp.where(lane >= 96, prior, row), 32, axis=1)
                    odd = pltpu.roll(jnp.where(lane < 32, later, row), 96, axis=1)
                    target[
                        pl.ds(pl.multiple_of((pairs * d + m) * 16, 16), 16),
                        a * LANES : (a + 1) * LANES,
                    ] = jnp.concatenate([even, odd], axis=0).astype(BF16)

        def at_pair(m):
            return pl.ds(pl.multiple_of(m * 2 * tiles, 2 * tiles), 2 * tiles)

        def far_block(block, target=None):
            pl.when(has_far)(lambda: block(far))
            if target is not None:

                @pl.when(jnp.logical_not(has_far))
                def _():
                    at_far = pl.ds(pl.multiple_of(far * pairs * 16, pairs * 16), pairs * 16)
                    target[at_far, :] = jnp.zeros((pairs * 16, 2 * LANES), BF16)

        def groups(count, step, far_ready):
            @pl.loop(0, count)
            def _(i):
                pl.when(i == 1)(far_ready)
                step(near // 2 * (count - 1) + i * (1 - near))

        def adjoint(out, far_ready):
            acc[...] = jnp.zeros_like(acc)

            def one(kk):
                lhs = jnp.concatenate(
                    [
                        win_adj[pl.ds(pl.multiple_of((group * kk + u) * 16, 16), pairs * 16), :]
                        for u in range(group)
                    ],
                    axis=1,
                )
                first = pl.multiple_of(2 * group * kk * LANES, LANES)
                rhs = jnp.concatenate(
                    [
                        band_adj[pl.ds(first + LANES, 2 * group * LANES), :],
                        band_adj[pl.ds(first, 2 * group * LANES), :],
                    ],
                    axis=1,
                )
                acc[...] += jnp.dot(lhs, rhs, preferred_element_type=F32)

            groups(steps // group, one, far_ready)

            def finish(m, total):
                for b in range(2):
                    cols = slice(b * LANES, (b + 1) * LANES)
                    even = acc[pl.ds(pl.multiple_of(m * 16, 16), 8), cols]
                    odd = acc[pl.ds(pl.multiple_of(m * 16 + 8, 8), 8), cols]
                    values = (
                        jnp.where(left_half, even, pltpu.roll(odd, 64, axis=1)),
                        jnp.where(left_half, pltpu.roll(even, 64, axis=1), odd),
                    )
                    for t in range(tools):
                        at_r = pl.ds(pl.multiple_of((t * rows + 2 * m + b) * tiles, tiles), tiles)
                        value = allowed[at_r, :] * values[t]
                        out[at_r, :] = value
                        total = total + value * value
                return total

            return lax.fori_loop(0, pairs, finish, jnp.zeros((SUB, LANES), F32), unroll=4)

        def sum_stage(which, source, box, count, peer_of):
            def copy_to(step):
                return pltpu.make_async_remote_copy(
                    src_ref=msg.at[source],
                    dst_ref=box.at[step - 1],
                    send_sem=sum_send.at[which],
                    recv_sem=sum_recv.at[which],
                    device_id=peer_of(step),
                    device_id_type=MESH,
                )

            for step in range(1, count):
                copy_to(step).start()

            all_of = pltpu.make_async_remote_copy(
                src_ref=box,
                dst_ref=box,
                send_sem=sum_send.at[which],
                recv_sem=sum_recv.at[which],
                device_id=peer_of(1),
                device_id_type=MESH,
            )
            return all_of

        def total_of(first, beside_plane, beside_line):
            stage = sum_stage(first, first, box_a.at[first // 2], plane_count, plane_peer)
            beside_plane()
            stage.wait_recv()
            msg[first + 1] = msg[first] + jnp.sum(box_a[first // 2], axis=0)
            other = sum_stage(first + 1, first + 1, box_b.at[first // 2], line_count, line_peer)
            beside_line()
            other.wait_recv()
            everything = msg[first + 1] + jnp.sum(box_b[first // 2], axis=0)
            return jnp.sum(everything, axis=1, keepdims=True), (stage, other)

        def first_block(d):
            first_halo[1](d)
            edge[...] = low_edge_in[d].astype(F32)
            if isinstance(d, int):
                assemble(win_adj, d, lambda m: masked[d, at_pair(m), :])
            else:
                assemble(win_adj, d, lambda m: low_in[d, at_pair(m), :].astype(F32))

        first_block(1)
        first_block(near)
        rad_wait(0)
        rad_send(1)

        def first_far():
            far_block(first_block, win_adj)

        gamma_part = adjoint(gradient, first_far)
        grad_low[...] = gradient[...].astype(BF16)
        for side, tile in ((0, tiles - 1), (1, 0)):
            grad_edge_out[side] = gradient[pl.ds(tile, tools * rows, stride=tiles), :].astype(BF16)
        for grad_halo in grad_halos:
            grad_halo[0]()
        meet_wait(0)
        meet_send(1)
        rad_wait(1)
        rad_send(2)

        for t in range(tools):

            @pl.loop(0, extent + 1, unroll=5)
            def _(q, t=t):
                at_q = pl.ds(pl.multiple_of((q + 2) * LANES, LANES), LANES)
                band_fwd[t, at_q, :] = toeplitz(head_fwd[t, pl.ds(q, 1), :], extent + 1, 1)

        acc_fwd[...] = jnp.zeros_like(acc_fwd)
        for t in range(tools):

            def grad_block(d, t=t):
                grad_halos[t][1](d)
                edge[...] = grad_edge_in[d, :, t * rows : (t + 1) * rows, :].astype(F32)

                def mine(m):
                    return pl.ds(pl.multiple_of(t * field + m * 16, 16), 16)

                if isinstance(d, int):
                    assemble(win_fwd.at[t], d, lambda m: gradient[mine(m), :])
                else:
                    assemble(win_fwd.at[t], d, lambda m: grad_in[d, mine(m), :].astype(F32))

            def one(kk, t=t):
                def rows_of(u):
                    return jnp.concatenate(
                        [
                            win_fwd[t, pl.ds(pl.multiple_of((group_fwd * kk + u + 2 * m) * 16, 16), 16), :]
                            for m in range(quads)
                        ],
                        axis=0,
                    )

                lhs = jnp.concatenate([rows_of(u) for u in range(group_fwd)], axis=1)
                first = pl.multiple_of(2 * group_fwd * kk * LANES, LANES)
                span = 2 * group_fwd * LANES
                rhs = jnp.concatenate(
                    [band_fwd[t, pl.ds(first + 2 * LANES, span), :], band_fwd[t, pl.ds(first, span), :]],
                    axis=1,
                )
                acc_fwd[...] += jnp.dot(lhs, rhs, preferred_element_type=F32)

            grad_block(1)
            grad_block(near)
            groups(steps_fwd // group_fwd, one, lambda t=t, block=grad_block: far_block(block, win_fwd.at[t]))
            if t == 0:
                masked_halo[0]()
                for step in range(2, rad_meetings):
                    if step > 2:
                        rad_send(step)
                    rad_wait(step)
                cross_send(0)

        @pl.loop(0, quads, unroll=4)
        def _(m):
            for h in range(2):
                cols = slice(h * LANES, (h + 1) * LANES)
                even = acc_fwd[pl.ds(pl.multiple_of(m * 16, 16), 8), cols]
                odd = acc_fwd[pl.ds(pl.multiple_of(m * 16 + 8, 8), 8), cols]
                top = jnp.where(left_half, even, pltpu.roll(odd, 64, axis=1))
                low = jnp.where(left_half, pltpu.roll(even, 64, axis=1), odd)
                at_m = at_pair(2 * m + h)
                part[at_m, :] = inside[at_m, :] * jnp.concatenate([top, low], axis=0)

        tool_copies = []
        for step in range(1, tool_count):
            tool_copies.append(
                pltpu.make_async_remote_copy(
                    src_ref=part,
                    dst_ref=part_in.at[step - 1],
                    send_sem=tool_sem.at[0, step - 1],
                    recv_sem=tool_sem.at[1, step - 1],
                    device_id={"az": az, "rad": rad, "tool": lax.rem(tool + step, tool_count)},
                    device_id_type=MESH,
                )
            )
        for copy in tool_copies:
            copy.start()
        meet_wait(1)
        meet_send(2)
        cross_wait(0)
        cross_send(1)
        for copy in tool_copies:
            copy.wait_recv()

        def join(m, total):
            at_m = at_pair(m)
            value = part[at_m, :]
            for step in range(1, tool_count):
                value = value + part_in[step - 1, at_m, :]
            removal[1, at_m, :] = value
            return total + value[:SUB] * value[:SUB] + value[SUB:] * value[SUB:]

        curvature_part = lax.fori_loop(0, pairs, join, jnp.zeros((SUB, LANES), F32), unroll=4)
        msg[0] = jnp.concatenate(
            [
                jnp.sum(gamma_part, axis=0, keepdims=True),
                jnp.sum(curvature_part, axis=0, keepdims=True),
            ],
            axis=0,
        )

        def edges():
            for side, tile in ((0, tiles - 1), (1, 0)):
                removal_edge_out[side] = removal[1, pl.ds(tile, rows, stride=tiles), :]
            dwell_copy.wait()
            meet_last()

        cross_wait(1)
        sums, stages = total_of(0, edges, removal_halo[0])
        gamma = sums[0:1]
        curvature = sums[1:2] * (1.0 / tool_count)
        step_size = gamma / (curvature + EPSILON)

        def second_block(d):
            masked_halo[1](d)
            removal_halo[1](d)
            edge[...] = masked_edge[d] - step_size * removal_edge[d]
            assemble(
                win_adj, d, lambda m: masked[d, at_pair(m), :] - step_size * removal[d, at_pair(m), :]
            )

        second_block(1)
        second_block(near)
        new_part = adjoint(gradient_new, lambda: far_block(second_block))
        new_row = jnp.sum(new_part, axis=0, keepdims=True)
        msg[2] = jnp.concatenate([new_row, new_row], axis=0)

        def dwell_output():
            for t in range(tools):
                for c in range(tiles):
                    cols = slice(c * LANES, (c + 1) * LANES)
                    step_of = gradient[pl.ds(t * field + c, rows, stride=tiles), :]
                    grad_natural[t, :, cols] = step_of
                    dwell_out[t, :, cols] = dwell_v[t, :, cols] + step_size * step_of

        def residual_output():
            for t in range(tools):
                for c in range(tiles):
                    from_c = pl.ds(t * field + c, rows, stride=tiles)
                    direction_out[t, :, c * LANES : (c + 1) * LANES] = gradient_new[from_c, :]
            for c in range(share_tiles):
                from_c = pl.ds(tool * share_tiles + c, rows, stride=tiles)
                residual_out[:, c * LANES : (c + 1) * LANES] = (
                    whole[from_c, :] - step_size * removal[1, from_c, :]
                )

        new_sums, new_stages = total_of(2, dwell_output, residual_output)
        ratio = new_sums[0:1] / (gamma + EPSILON)
        for t in range(tools):
            direction_out[t] = direction_out[t] + ratio * grad_natural[t]

        for phase in (first_halo, masked_halo, *grad_halos, removal_halo):
            phase[2]()
        for copy in tool_copies:
            copy.wait_send()
        for stage in stages + new_stages:
            stage.wait_send()

    hbm_spec = pl.BlockSpec(memory_space=pltpu.HBM)
    scratch = [
        ((rows, width), F32),
        (dwell_shape, F32),
        ((field, LANES), F32),
        ((3, field, LANES), F32),
        ((3, 2, rows, LANES), F32),
        ((2, rows, LANES), F32),
        ((field, LANES), BF16),
        ((2, rows, LANES), BF16),
        ((3, field, LANES), BF16),
        ((3, 2, rows, LANES), BF16),
        ((field, LANES), F32),
        ((tools * field, LANES), F32),
        ((extent, LANES), F32),
        ((tools, extent + 8, LANES), F32),
        ((tools, extent + 8, LANES), F32),
        ((2, LANES, LANES), F32),
        (((extent + 3) * LANES, LANES), BF16),
        ((tools, (extent + 6) * LANES, LANES), BF16),
        ((3 * pairs * 16, 2 * LANES), BF16),
        ((tools, 3 * pairs * 16, 2 * LANES), BF16),
        ((pairs * 16, 2 * LANES), F32),
        ((quads * 16, 2 * LANES), F32),
        ((tools * field, LANES), F32),
        ((tools * field, LANES), BF16),
        ((2, tools * rows, LANES), BF16),
        ((3, tools * field, LANES), BF16),
        ((3, 2, tools * rows, LANES), BF16),
        ((field, LANES), F32),
        ((tool_count - 1, field, LANES), F32),
        ((3, field, LANES), F32),
        ((2, rows, LANES), F32),
        ((3, 2, rows, LANES), F32),
        ((2, rows, LANES), F32),
        ((tools * field, LANES), F32),
        (dwell_shape, F32),
        ((4, 2, LANES), F32),
        ((2, plane_count - 1, 2, LANES), F32),
        ((2, line_count - 1, 2, LANES), F32),
    ]
    return pl.pallas_call(
        body,
        out_shape=(
            pltpu.VMEM(dwell_shape, F32),
            pltpu.VMEM((rows, share), F32),
            pltpu.VMEM(dwell_shape, F32),
        ),
        in_specs=[hbm_spec] * 6,
        out_specs=(pl.BlockSpec(memory_space=pltpu.VMEM),) * 3,
        scratch_shapes=[
            pltpu.VMEM(influence_shape, BF16),
            pltpu.SMEM((rows,), jnp.int32),
            pltpu.SMEM((rows,), jnp.int32),
            pltpu.VMEM((tools, rows, words), jnp.int32),
        ]
        + [pltpu.VMEM(shape, dtype) for shape, dtype in scratch]
        + [
            pltpu.SemaphoreType.DMA((9,)),
            pltpu.SemaphoreType.DMA((5, 9)),
            pltpu.SemaphoreType.DMA((5, 9)),
            pltpu.SemaphoreType.DMA((2, max(tool_count - 1, 1))),
            pltpu.SemaphoreType.REGULAR((max(meetings_of(line_count), 1),)),
            pltpu.SemaphoreType.REGULAR(((rad_count - 1).bit_length() + 2,)),
            pltpu.SemaphoreType.DMA((4,)),
            pltpu.SemaphoreType.DMA((4,)),
        ],
        compiler_params=pltpu.CompilerParams(
            collective_id=0, has_side_effects=True, vmem_limit_bytes=24 * 1024 * 1024
        ),
        name="cgls",
    )


def hand_on(results):
    count = len(results)

    def body(*refs):
        sem = refs[-1]
        copies = [
            pltpu.make_async_copy(refs[i], refs[count + i], sem.at[i]) for i in range(count)
        ]
        for copy in copies:
            copy.start()
        for copy in copies:
            copy.wait()

    return pl.pallas_call(
        body,
        out_shape=tuple(jax.ShapeDtypeStruct(x.shape, x.dtype) for x in results),
        in_specs=[pl.BlockSpec(memory_space=pl.ANY)] * count,
        out_specs=(pl.BlockSpec(memory_space=pltpu.HBM),) * count,
        scratch_shapes=[pltpu.SemaphoreType.DMA((count,))],
        name="hand_on",
    )(*(pltpu.with_memory_space_constraint(x, pltpu.VMEM) for x in results))


def solution(mesh):
    def per_device(dwell, residual, influence, cycle_start, cycle_end, allowed_bits):
        call = build(
            dwell.shape,
            influence.shape,
            allowed_bits.shape[-1],
            mesh.shape["az"],
            mesh.shape["rad"],
            mesh.shape["tool"],
        )
        given = (dwell, residual, influence, cycle_start, cycle_end, allowed_bits)
        return hand_on(call(*(pltpu.with_memory_space_constraint(x, pltpu.HBM) for x in given)))

    in_specs = (
        P("tool", "rad", "az"),
        P("rad", "az"),
        P("tool", None, None),
        P("rad"),
        P("rad"),
        P("tool", "rad", "az"),
    )
    out_specs = (P("tool", "rad", "az"), P("rad", ("az", "tool")), P("tool", "rad", "az"))
    return jax.shard_map(
        per_device, mesh=mesh, in_specs=in_specs, out_specs=out_specs, check_vma=False
    )
```

```python
import jax
import jax.numpy as jnp
from jax import lax
from jax.experimental import pallas as pl
from jax.experimental.pallas import tpu as pltpu
from jax.sharding import PartitionSpec as P

EPSILON = 1e-06
MESH = pl.DeviceIdType.MESH
F32 = jnp.float32
BF16 = jnp.bfloat16
LANES = 128
SUB = 8


def meetings_of(line_count):
    return max(line_count // 2, 1).bit_length() - 1


def build(dwell_shape, influence_shape, words, az_count, rad_count, tool_count):
    tools, rows, width = dwell_shape
    extent = influence_shape[-1]
    tiles = width // LANES
    assert tiles == SUB and extent == 64 and rows == 32
    pairs = rows // 2
    field = rows * tiles
    steps = extent // 2 + 1
    group = 11
    quads, steps_fwd, group_fwd = rows // 4, extent // 2 + 2, 17
    assert steps % group == 0 and steps_fwd % group_fwd == 0
    plane_count = 2 * rad_count * tool_count
    line_count = az_count // 2
    for count in (az_count, rad_count, tool_count):
        assert count & (count - 1) == 0
    share = width // tool_count
    share_tiles = share // LANES

    def body(
        dwell_hbm,
        residual_hbm,
        influence_hbm,
        start_hbm,
        end_hbm,
        bits_hbm,
        dwell_out,
        residual_out,
        direction_out,
        influence_ref,
        start_ref,
        end_ref,
        bits_ref,
        natural,
        dwell_v,
        whole,
        masked,
        masked_edge,
        masked_edge_out,
        low_out,
        low_edge_out,
        low_in,
        low_edge_in,
        inside,
        allowed,
        head_adj,
        head_fwd,
        head_two,
        keep,
        band_adj,
        band_fwd,
        win_adj,
        win_fwd,
        acc,
        acc_fwd,
        gradient,
        grad_low,
        grad_edge_out,
        grad_in,
        grad_edge_in,
        part,
        part_in,
        removal,
        removal_edge_out,
        removal_edge,
        edge,
        gradient_new,
        grad_natural,
        msg,
        box_a,
        box_b,
        local_sem,
        halo_send,
        halo_recv,
        tool_sem,
        meet,
        plane_meet,
        sum_send,
        sum_recv,
    ):
        az, rad, tool = lax.axis_index("az"), lax.axis_index("rad"), lax.axis_index("tool")
        lane = lax.broadcasted_iota(jnp.int32, (SUB, LANES), 1)
        sub = lax.broadcasted_iota(jnp.int32, (SUB, LANES), 0)
        left_half = lane < LANES // 2

        residual_copy = pltpu.make_async_copy(residual_hbm, natural, local_sem.at[0])
        start_copy = pltpu.make_async_copy(start_hbm, start_ref, local_sem.at[5])
        end_copy = pltpu.make_async_copy(end_hbm, end_ref, local_sem.at[6])
        influence_copy = pltpu.make_async_copy(influence_hbm, influence_ref, local_sem.at[7])
        bits_copy = pltpu.make_async_copy(bits_hbm, bits_ref, local_sem.at[8])
        dwell_copy = pltpu.make_async_copy(dwell_hbm, dwell_v, local_sem.at[1])

        def at(dr, da):
            return {
                "az": lax.rem(az + da + az_count, az_count),
                "rad": rad + dr,
                "tool": tool,
            }

        def plane_peer(step):
            return {
                "az": az ^ (step % 2),
                "rad": rad ^ (step // (2 * tool_count)),
                "tool": tool ^ (step // 2 % tool_count),
            }

        def line_peer(step):
            return {"az": az ^ (2 * step), "rad": rad, "tool": tool}

        has_up, has_down = rad > 0, rad < rad_count - 1

        barrier = pltpu.get_barrier_semaphore()

        def greet(peer):
            pl.semaphore_signal(barrier, inc=1, device_id=peer, device_id_type=MESH)

        for da in (1, -1, 2, -2):
            greet(at(0, da))
        for step in range(1, tool_count):
            greet({"az": az, "rad": rad, "tool": tool ^ step})
        for there, dr in ((has_up, -1), (has_down, 1)):

            @pl.when(there)
            def _(dr=dr):
                for da in (0, 1, -1):
                    greet(at(dr, da))

        for copy in (residual_copy, start_copy, end_copy, influence_copy, bits_copy, dwell_copy):
            copy.start()

        residual_copy.wait()
        for c in range(tiles):
            whole[pl.ds(c, rows, stride=tiles), :] = natural[:, c * LANES : (c + 1) * LANES]
        start_copy.wait()
        end_copy.wait()
        column = az * width + sub * LANES + lane

        @pl.loop(0, rows, unroll=4)
        def _(r):
            at_r = pl.ds(pl.multiple_of(r * tiles, tiles), tiles)
            valid = ((column >= start_ref[r]) & (column < end_ref[r])).astype(F32)
            inside[at_r, :] = valid
            masked[1, at_r, :] = valid * whole[at_r, :]

        low_out[...] = masked[1].astype(BF16)
        for side, tile in ((0, tiles - 1), (1, 0)):
            tile_of = masked[1, pl.ds(tile, rows, stride=tiles), :]
            masked_edge_out[side] = tile_of
            low_edge_out[side] = tile_of.astype(BF16)

        beside = has_up.astype(jnp.int32) + has_down.astype(jnp.int32)
        pl.semaphore_wait(barrier, 3 + tool_count + 3 * beside)

        rad_meetings = (rad_count - 1).bit_length()

        def tell(which, peer):
            pl.semaphore_signal(plane_meet.at[which], inc=1, device_id=peer, device_id_type=MESH)

        def rad_send(step):
            if step < rad_meetings:
                reach = 1 << step
                pl.when(rad >= reach)(lambda: tell(step, at(-reach, 0)))
                pl.when(rad + reach < rad_count)(lambda: tell(step, at(reach, 0)))

        def rad_wait(step):
            if step < rad_meetings:
                reach = 1 << step
                known = (rad >= reach).astype(jnp.int32) + (rad + reach < rad_count).astype(jnp.int32)
                pl.semaphore_wait(plane_meet.at[step], known)

        def cross_send(step):
            if step == 0:
                for other in range(1, tool_count):
                    tell(rad_meetings, {"az": az, "rad": rad, "tool": tool ^ other})
            tell(rad_meetings + step, {"az": az ^ 1, "rad": rad, "tool": tool})

        def cross_wait(step):
            pl.semaphore_wait(plane_meet.at[rad_meetings + step], 1 if step else tool_count)

        meetings = meetings_of(line_count)

        def meet_send(step):
            if step < meetings:
                for da in (2 << step, -(2 << step)):
                    pl.semaphore_signal(meet.at[step], inc=1, device_id=at(0, da), device_id_type=MESH)

        def meet_wait(step):
            if step < meetings:
                pl.semaphore_wait(meet.at[step], 2)

        def meet_last():
            for step in range(2, meetings):
                if step > 2:
                    meet_send(step)
                meet_wait(step)

        def halo(phase, mid_src, mid_dst, edge_src, edge_dst):
            sides = ((1, 0),) if mid_dst is not None else ()
            sides += ((0, 1), (2, -1)) if edge_dst is not None else ()

            def copy_of(d, side, da):
                return pltpu.make_async_remote_copy(
                    src_ref=mid_src if side == 1 else edge_src.at[side // 2],
                    dst_ref=mid_dst(d) if side == 1 else edge_dst.at[d, side // 2],
                    send_sem=halo_send.at[phase, 3 * d + side],
                    recv_sem=halo_recv.at[phase, 3 * d + side],
                    device_id=at(1 - d, da),
                    device_id_type=MESH,
                )

            def of_block(d, act, own=False):
                for side, da in sides:
                    if not (own and side == 1):
                        act(copy_of(d, side, da))

            def to_all(act):
                pl.when(has_down)(lambda: of_block(0, act))
                pl.when(has_up)(lambda: of_block(2, act))
                of_block(1, act, own=True)

            def start():
                to_all(lambda copy: copy.start())

            def wait_recv(d):
                of_block(d, lambda copy: copy.wait_recv(), own=isinstance(d, int))

            def wait_send():
                to_all(lambda copy: copy.wait_send())

            return start, wait_recv, wait_send

        first_halo = halo(0, low_out, lambda d: low_in.at[d], low_edge_out, low_edge_in)
        masked_halo = halo(1, masked.at[1], lambda d: masked.at[d], masked_edge_out, masked_edge)
        removal_halo = halo(3, removal.at[1], lambda d: removal.at[d], removal_edge_out, removal_edge)

        def grad_phase(t):
            mine = pl.ds(t * field, field)
            edges_of = (grad_edge_out, grad_edge_in) if t == 0 else (None, None)
            return halo(4 if t else 2, grad_low.at[mine], lambda d: grad_in.at[d, mine], *edges_of)

        grad_halos = [grad_phase(t) for t in range(tools)]
        near = 2 - 2 * lax.rem(rad, 2)
        far = 2 - near
        has_far = jnp.where(near == 2, rad, rad_count - 1 - rad) > 0

        first_halo[0]()
        meet_send(0)
        rad_send(0)

        influence_copy.wait()
        j_of = lax.broadcasted_iota(jnp.int32, (extent, LANES), 0)
        l_of = lax.broadcasted_iota(jnp.int32, (extent, LANES), 1)

        def spread(rows_of, where_j):
            return jnp.dot(rows_of, (l_of == where_j).astype(BF16), preferred_element_type=F32)

        head_adj[...] = spread(influence_ref[0], j_of) + spread(influence_ref[1], extent + j_of)
        head_fwd[...] = jnp.zeros_like(head_fwd)
        head_two[...] = jnp.zeros_like(head_two)
        for t in range(tools):
            head_fwd[t, 0:extent, :] = spread(influence_ref[t], extent - 1 - j_of)
            head_two[t, 1 : extent + 1, :] = spread(influence_ref[t], 2 * extent - 1 - j_of)
        head_fwd[...] = head_fwd[...] + head_two[...]
        c_of = lax.broadcasted_iota(jnp.int32, (LANES, LANES), 0)
        o_of = lax.broadcasted_iota(jnp.int32, (LANES, LANES), 1)
        low_side = o_of < extent
        off = o_of - c_of
        adj_keep = (low_side & (off >= -extent) & (off < 0)) | (~low_side & (off >= 0) & (off < extent))
        fwd_keep = (low_side & (off > -extent) & (off <= 0)) | (~low_side & (off > 0) & (off <= extent))
        keep[0] = adj_keep.astype(F32)
        keep[1] = fwd_keep.astype(F32)
        blank = jnp.zeros((LANES, LANES), BF16)
        band_adj[0:LANES, :] = blank
        band_adj[LANES : 2 * LANES, :] = blank
        band_adj[(extent + 2) * LANES : (extent + 3) * LANES, :] = blank
        for t in range(tools):
            band_fwd[t, 0 : 2 * LANES, :] = jnp.zeros((2 * LANES, LANES), BF16)
            band_fwd[t, (extent + 3) * LANES :, :] = jnp.zeros((3 * LANES, LANES), BF16)

        def toeplitz(head, shift, which):
            square = jnp.broadcast_to(head, (LANES, LANES))
            turned = pltpu.roll(square, shift, axis=1, stride=1, stride_axis=0)
            return (turned * keep[which]).astype(BF16)

        @pl.loop(0, extent, unroll=4)
        def _(i):
            at_i = pl.ds(pl.multiple_of((extent + 1 - i) * LANES, LANES), LANES)
            band_adj[at_i, :] = toeplitz(head_adj[pl.ds(i, 1), :], extent, 0)

        k_of = lax.broadcasted_iota(jnp.int32, (words, LANES), 0)
        b_of = lax.broadcasted_iota(jnp.int32, (words, LANES), 1)
        bits_copy.wait()
        word = bits_ref[...].reshape(tools * rows, words)
        low_byte = (word & 255).astype(F32).astype(BF16)
        high_byte = (word >> 8).astype(F32).astype(BF16)
        for c in range(tiles):
            mine = k_of == c * (LANES // 16) + b_of // 16
            upper = b_of % 16 >= 8
            byte = jnp.dot(low_byte, (mine & ~upper).astype(BF16), preferred_element_type=F32)
            byte += jnp.dot(high_byte, (mine & upper).astype(BF16), preferred_element_type=F32)
            bit_at = lax.broadcasted_iota(jnp.int32, byte.shape, 1) % 8
            allowed[pl.ds(c, tools * rows, stride=tiles), :] = (
                (byte.astype(jnp.int32) >> bit_at) & 1
            ).astype(F32)

        def assemble(target, d, two_rows):
            @pl.loop(0, pairs, unroll=True)
            def _(m):
                both = two_rows(m)
                for a in range(2):
                    row = both[a * tiles : (a + 1) * tiles]
                    before = jnp.broadcast_to(edge[0, pl.ds(2 * m + a, 1), :], (SUB, LANES))
                    after = jnp.broadcast_to(edge[1, pl.ds(2 * m + a, 1), :], (SUB, LANES))
                    prior = jnp.where(sub == 0, before, pltpu.roll(row, 1, axis=0))
                    later = jnp.where(sub == SUB - 1, after, pltpu.roll(row, SUB - 1, axis=0))
                    even = pltpu.roll(jnp.where(lane >= 96, prior, row), 32, axis=1)
                    odd = pltpu.roll(jnp.where(lane < 32, later, row), 96, axis=1)
                    target[
                        pl.ds(pl.multiple_of((pairs * d + m) * 16, 16), 16),
                        a * LANES : (a + 1) * LANES,
                    ] = jnp.concatenate([even, odd], axis=0).astype(BF16)

        def at_pair(m):
            return pl.ds(pl.multiple_of(m * 2 * tiles, 2 * tiles), 2 * tiles)

        def far_block(block, target=None):
            pl.when(has_far)(lambda: block(far))
            if target is not None:

                @pl.when(jnp.logical_not(has_far))
                def _():
                    at_far = pl.ds(pl.multiple_of(far * pairs * 16, pairs * 16), pairs * 16)
                    target[at_far, :] = jnp.zeros((pairs * 16, 2 * LANES), BF16)

        def groups(count, step, far_ready):
            @pl.loop(0, count)
            def _(i):
                pl.when(i == 1)(far_ready)
                step(near // 2 * (count - 1) + i * (1 - near))

        def adjoint(out, far_ready):
            def one(kk):
                lhs = jnp.concatenate(
                    [
                        win_adj[pl.ds(pl.multiple_of((group * kk + u) * 16, 16), pairs * 16), :]
                        for u in range(group)
                    ],
                    axis=1,
                )
                first = pl.multiple_of(2 * group * kk * LANES, LANES)
                rhs = jnp.concatenate(
                    [
                        band_adj[pl.ds(first + LANES, 2 * group * LANES), :],
                        band_adj[pl.ds(first, 2 * group * LANES), :],
                    ],
                    axis=1,
                )
                acc[...] += jnp.dot(lhs, rhs, preferred_element_type=F32)

            groups(steps // group, one, far_ready)

            def finish(m, total):
                for b in range(2):
                    cols = slice(b * LANES, (b + 1) * LANES)
                    even = acc[pl.ds(pl.multiple_of(m * 16, 16), 8), cols]
                    odd = acc[pl.ds(pl.multiple_of(m * 16 + 8, 8), 8), cols]
                    values = (
                        jnp.where(left_half, even, pltpu.roll(odd, 64, axis=1)),
                        jnp.where(left_half, pltpu.roll(even, 64, axis=1), odd),
                    )
                    for t in range(tools):
                        at_r = pl.ds(pl.multiple_of((t * rows + 2 * m + b) * tiles, tiles), tiles)
                        value = allowed[at_r, :] * values[t]
                        out[at_r, :] = value
                        total = total + value * value
                return total

            return lax.fori_loop(0, pairs, finish, jnp.zeros((SUB, LANES), F32), unroll=4)

        def sum_stage(which, source, box, count, peer_of):
            def copy_to(step):
                return pltpu.make_async_remote_copy(
                    src_ref=msg.at[source],
                    dst_ref=box.at[step - 1],
                    send_sem=sum_send.at[which],
                    recv_sem=sum_recv.at[which],
                    device_id=peer_of(step),
                    device_id_type=MESH,
                )

            for step in range(1, count):
                copy_to(step).start()

            all_of = pltpu.make_async_remote_copy(
                src_ref=box,
                dst_ref=box,
                send_sem=sum_send.at[which],
                recv_sem=sum_recv.at[which],
                device_id=peer_of(1),
                device_id_type=MESH,
            )
            return all_of

        def total_of(first, beside_plane, beside_line):
            stage = sum_stage(first, first, box_a.at[first // 2], plane_count, plane_peer)
            beside_plane()
            stage.wait_recv()
            msg[first + 1] = msg[first] + jnp.sum(box_a[first // 2], axis=0)
            other = sum_stage(first + 1, first + 1, box_b.at[first // 2], line_count, line_peer)
            beside_line()
            other.wait_recv()
            everything = msg[first + 1] + jnp.sum(box_b[first // 2], axis=0)
            return jnp.sum(everything, axis=1, keepdims=True), (stage, other)

        def first_block(d):
            first_halo[1](d)
            edge[...] = low_edge_in[d].astype(F32)
            if isinstance(d, int):
                assemble(win_adj, d, lambda m: masked[d, at_pair(m), :])
            else:
                assemble(win_adj, d, lambda m: low_in[d, at_pair(m), :].astype(F32))

        acc[...] = jnp.zeros_like(acc)
        first_block(1)
        first_block(near)
        rad_wait(0)
        rad_send(1)

        def first_far():
            far_block(first_block, win_adj)

        gamma_part = adjoint(gradient, first_far)
        for side, tile in ((0, tiles - 1), (1, 0)):
            grad_edge_out[side] = gradient[pl.ds(tile, tools * rows, stride=tiles), :].astype(BF16)
        for t in range(tools):
            mine = slice(t * field, (t + 1) * field)
            grad_low[mine, :] = gradient[mine, :].astype(BF16)
            grad_halos[t][0]()
        meet_wait(0)
        meet_send(1)
        rad_wait(1)
        rad_send(2)

        for t in range(tools):

            @pl.loop(0, extent + 1, unroll=5)
            def _(q, t=t):
                at_q = pl.ds(pl.multiple_of((q + 2) * LANES, LANES), LANES)
                band_fwd[t, at_q, :] = toeplitz(head_fwd[t, pl.ds(q, 1), :], extent + 1, 1)

        acc_fwd[...] = jnp.zeros_like(acc_fwd)
        for t in range(tools):

            def grad_block(d, t=t):
                grad_halos[t][1](d)
                edge[...] = grad_edge_in[d, :, t * rows : (t + 1) * rows, :].astype(F32)

                def mine(m):
                    return pl.ds(pl.multiple_of(t * field + m * 16, 16), 16)

                if isinstance(d, int):
                    assemble(win_fwd.at[t], d, lambda m: gradient[mine(m), :])
                else:
                    assemble(win_fwd.at[t], d, lambda m: grad_in[d, mine(m), :].astype(F32))

            def one(kk, t=t):
                def rows_of(u):
                    return jnp.concatenate(
                        [
                            win_fwd[t, pl.ds(pl.multiple_of((group_fwd * kk + u + 2 * m) * 16, 16), 16), :]
                            for m in range(quads)
                        ],
                        axis=0,
                    )

                lhs = jnp.concatenate([rows_of(u) for u in range(group_fwd)], axis=1)
                first = pl.multiple_of(2 * group_fwd * kk * LANES, LANES)
                span = 2 * group_fwd * LANES
                rhs = jnp.concatenate(
                    [band_fwd[t, pl.ds(first + 2 * LANES, span), :], band_fwd[t, pl.ds(first, span), :]],
                    axis=1,
                )
                acc_fwd[...] += jnp.dot(lhs, rhs, preferred_element_type=F32)

            grad_block(1)
            grad_block(near)
            groups(steps_fwd // group_fwd, one, lambda t=t, block=grad_block: far_block(block, win_fwd.at[t]))
            if t == 0:
                masked_halo[0]()
                for step in range(2, rad_meetings):
                    if step > 2:
                        rad_send(step)
                    rad_wait(step)
                cross_send(0)

        @pl.loop(0, quads, unroll=4)
        def _(m):
            for h in range(2):
                cols = slice(h * LANES, (h + 1) * LANES)
                even = acc_fwd[pl.ds(pl.multiple_of(m * 16, 16), 8), cols]
                odd = acc_fwd[pl.ds(pl.multiple_of(m * 16 + 8, 8), 8), cols]
                top = jnp.where(left_half, even, pltpu.roll(odd, 64, axis=1))
                low = jnp.where(left_half, pltpu.roll(even, 64, axis=1), odd)
                at_m = at_pair(2 * m + h)
                part[at_m, :] = inside[at_m, :] * jnp.concatenate([top, low], axis=0)

        tool_copies = []
        for step in range(1, tool_count):
            tool_copies.append(
                pltpu.make_async_remote_copy(
                    src_ref=part,
                    dst_ref=part_in.at[step - 1],
                    send_sem=tool_sem.at[0, step - 1],
                    recv_sem=tool_sem.at[1, step - 1],
                    device_id={"az": az, "rad": rad, "tool": lax.rem(tool + step, tool_count)},
                    device_id_type=MESH,
                )
            )
        for copy in tool_copies:
            copy.start()
        meet_wait(1)
        meet_send(2)
        cross_wait(0)
        cross_send(1)
        for copy in tool_copies:
            copy.wait_recv()

        def join(m, total):
            at_m = at_pair(m)
            value = part[at_m, :]
            for step in range(1, tool_count):
                value = value + part_in[step - 1, at_m, :]
            removal[1, at_m, :] = value
            return total + value[:SUB] * value[:SUB] + value[SUB:] * value[SUB:]

        curvature_part = lax.fori_loop(0, pairs, join, jnp.zeros((SUB, LANES), F32), unroll=4)
        msg[0] = jnp.concatenate(
            [
                jnp.sum(gamma_part, axis=0, keepdims=True),
                jnp.sum(curvature_part, axis=0, keepdims=True),
            ],
            axis=0,
        )

        def edges():
            for side, tile in ((0, tiles - 1), (1, 0)):
                removal_edge_out[side] = removal[1, pl.ds(tile, rows, stride=tiles), :]
            dwell_copy.wait()
            meet_last()
            acc[...] = jnp.zeros_like(acc)

        cross_wait(1)
        sums, stages = total_of(0, edges, removal_halo[0])
        gamma = sums[0:1]
        curvature = sums[1:2] * (1.0 / tool_count)
        step_size = gamma / (curvature + EPSILON)

        def second_block(d):
            masked_halo[1](d)
            removal_halo[1](d)
            edge[...] = masked_edge[d] - step_size * removal_edge[d]
            assemble(
                win_adj, d, lambda m: masked[d, at_pair(m), :] - step_size * removal[d, at_pair(m), :]
            )

        second_block(1)
        second_block(near)
        new_part = adjoint(gradient_new, lambda: far_block(second_block))
        new_row = jnp.sum(new_part, axis=0, keepdims=True)
        msg[2] = jnp.concatenate([new_row, new_row], axis=0)

        def dwell_output():
            for t in range(tools):
                for c in range(tiles):
                    cols = slice(c * LANES, (c + 1) * LANES)
                    step_of = gradient[pl.ds(t * field + c, rows, stride=tiles), :]
                    grad_natural[t, :, cols] = step_of
                    dwell_out[t, :, cols] = dwell_v[t, :, cols] + step_size * step_of

        def residual_output():
            for t in range(tools):
                for c in range(tiles):
                    from_c = pl.ds(t * field + c, rows, stride=tiles)
                    direction_out[t, :, c * LANES : (c + 1) * LANES] = gradient_new[from_c, :]
            for c in range(share_tiles):
                from_c = pl.ds(tool * share_tiles + c, rows, stride=tiles)
                residual_out[:, c * LANES : (c + 1) * LANES] = (
                    whole[from_c, :] - step_size * removal[1, from_c, :]
                )

        new_sums, new_stages = total_of(2, dwell_output, residual_output)
        ratio = new_sums[0:1] / (gamma + EPSILON)
        for t in range(tools):
            direction_out[t] = direction_out[t] + ratio * grad_natural[t]

        for phase in (first_halo, masked_halo, *grad_halos, removal_halo):
            phase[2]()
        for copy in tool_copies:
            copy.wait_send()
        for stage in stages + new_stages:
            stage.wait_send()

    hbm_spec = pl.BlockSpec(memory_space=pltpu.HBM)
    scratch = [
        ((rows, width), F32),
        (dwell_shape, F32),
        ((field, LANES), F32),
        ((3, field, LANES), F32),
        ((3, 2, rows, LANES), F32),
        ((2, rows, LANES), F32),
        ((field, LANES), BF16),
        ((2, rows, LANES), BF16),
        ((3, field, LANES), BF16),
        ((3, 2, rows, LANES), BF16),
        ((field, LANES), F32),
        ((tools * field, LANES), F32),
        ((extent, LANES), F32),
        ((tools, extent + 8, LANES), F32),
        ((tools, extent + 8, LANES), F32),
        ((2, LANES, LANES), F32),
        (((extent + 3) * LANES, LANES), BF16),
        ((tools, (extent + 6) * LANES, LANES), BF16),
        ((3 * pairs * 16, 2 * LANES), BF16),
        ((tools, 3 * pairs * 16, 2 * LANES), BF16),
        ((pairs * 16, 2 * LANES), F32),
        ((quads * 16, 2 * LANES), F32),
        ((tools * field, LANES), F32),
        ((tools * field, LANES), BF16),
        ((2, tools * rows, LANES), BF16),
        ((3, tools * field, LANES), BF16),
        ((3, 2, tools * rows, LANES), BF16),
        ((field, LANES), F32),
        ((tool_count - 1, field, LANES), F32),
        ((3, field, LANES), F32),
        ((2, rows, LANES), F32),
        ((3, 2, rows, LANES), F32),
        ((2, rows, LANES), F32),
        ((tools * field, LANES), F32),
        (dwell_shape, F32),
        ((4, 2, LANES), F32),
        ((2, plane_count - 1, 2, LANES), F32),
        ((2, line_count - 1, 2, LANES), F32),
    ]
    return pl.pallas_call(
        body,
        out_shape=(
            pltpu.VMEM(dwell_shape, F32),
            pltpu.VMEM((rows, share), F32),
            pltpu.VMEM(dwell_shape, F32),
        ),
        in_specs=[hbm_spec] * 6,
        out_specs=(pl.BlockSpec(memory_space=pltpu.VMEM),) * 3,
        scratch_shapes=[
            pltpu.VMEM(influence_shape, BF16),
            pltpu.SMEM((rows,), jnp.int32),
            pltpu.SMEM((rows,), jnp.int32),
            pltpu.VMEM((tools, rows, words), jnp.int32),
        ]
        + [pltpu.VMEM(shape, dtype) for shape, dtype in scratch]
        + [
            pltpu.SemaphoreType.DMA((9,)),
            pltpu.SemaphoreType.DMA((5, 9)),
            pltpu.SemaphoreType.DMA((5, 9)),
            pltpu.SemaphoreType.DMA((2, max(tool_count - 1, 1))),
            pltpu.SemaphoreType.REGULAR((max(meetings_of(line_count), 1),)),
            pltpu.SemaphoreType.REGULAR(((rad_count - 1).bit_length() + 2,)),
            pltpu.SemaphoreType.DMA((4,)),
            pltpu.SemaphoreType.DMA((4,)),
        ],
        compiler_params=pltpu.CompilerParams(
            collective_id=0, has_side_effects=True, vmem_limit_bytes=24 * 1024 * 1024
        ),
        name="cgls",
    )


def hand_on(results):
    count = len(results)

    def body(*refs):
        sem = refs[-1]
        copies = [
            pltpu.make_async_copy(refs[i], refs[count + i], sem.at[i]) for i in range(count)
        ]
        for copy in copies:
            copy.start()
        for copy in copies:
            copy.wait()

    return pl.pallas_call(
        body,
        out_shape=tuple(jax.ShapeDtypeStruct(x.shape, x.dtype) for x in results),
        in_specs=[pl.BlockSpec(memory_space=pl.ANY)] * count,
        out_specs=(pl.BlockSpec(memory_space=pltpu.HBM),) * count,
        scratch_shapes=[pltpu.SemaphoreType.DMA((count,))],
        name="hand_on",
    )(*(pltpu.with_memory_space_constraint(x, pltpu.VMEM) for x in results))


def solution(mesh):
    def per_device(dwell, residual, influence, cycle_start, cycle_end, allowed_bits):
        call = build(
            dwell.shape,
            influence.shape,
            allowed_bits.shape[-1],
            mesh.shape["az"],
            mesh.shape["rad"],
            mesh.shape["tool"],
        )
        given = (dwell, residual, influence, cycle_start, cycle_end, allowed_bits)
        return hand_on(call(*(pltpu.with_memory_space_constraint(x, pltpu.HBM) for x in given)))

    in_specs = (
        P("tool", "rad", "az"),
        P("rad", "az"),
        P("tool", None, None),
        P("rad"),
        P("rad"),
        P("tool", "rad", "az"),
    )
    out_specs = (P("tool", "rad", "az"), P("rad", ("az", "tool")), P("tool", "rad", "az"))
    return jax.shard_map(
        per_device, mesh=mesh, in_specs=in_specs, out_specs=out_specs, check_vma=False
    )
```
